512 devices in a mesh: fsdp: 2 (over core), ctx: 64 (over y, z), dp: 4 (over x).
Axes of the slice: x: 4, y: 4, z: 16, core: 2. Of those that a mesh axis runs over, the one named last changes fastest.
Arguments:
- query_stream: bfloat16 [1, 8192, 8192], P(None, 'ctx', ('fsdp', 'dp')), may hold values from -6 to 6
- key_stream: bfloat16 [1, 8192, 8192], P(None, 'ctx', ('fsdp', 'dp')), may hold values from -6 to 6
- value_stream: bfloat16 [1, 8192, 8192], P(None, 'ctx', ('fsdp', 'dp')), may hold values from -6 to 6
- document_starts: int32 [1, 8192], replicated, may hold values 0 or 1
- medium_taps: bfloat16 [512, 128], P(None, 'fsdp'), may hold values from -0.5 to 0.5
- modal_rate: bfloat16 [512, 16], P('fsdp', 'dp'), may hold values from 2.4288893e-06 to 0.032958984
- modal_residue: bfloat16 [512, 16], P('fsdp', 'dp'), may hold values from -4 to 4
- skip_gain: float32 [8192], P(('fsdp', 'dp')), may hold values from 0.5 to 1.5
Outputs:
- hyena_out: bfloat16 [1, 8192, 8192], P(None, 'ctx', ('fsdp', 'dp'))
The draws below stay inside these ranges and needn't reach their ends.
All inputs are finite; a program needn't handle non-finite values.
Results may differ from the reference program's by a relative error of at most 0.0085.
Values may be sent and summed in bfloat16 or wider, within the bound.
A program may use at most 64 MiB of HBM per device.

```python
import math
import jax
import jax.numpy as jnp
from jax import lax

D = 8192
TAPS = 128
ORDER = 16
GROUP_CH = 16
SEGMENTS = 1
SEQ = 8192
GROUPS = 512


def touch_ends(entries, stream_key, low, top_value):
    extent = entries.shape
    place = [jax.random.randint(jax.random.fold_in(stream_key, axis), (), 0, extent[axis]) for axis in range(len(extent))]
    entries = entries.at[tuple(place)].set(low)
    longest = extent.index(max(extent))
    place[longest] = (place[longest] + 1) % extent[longest]
    return entries.at[tuple(place)].set(top_value)


def block_scale(rng, dims, shards, least, largest):
    factor_of, own = 1.0, jax.random.fold_in(rng, 6)
    for position, parts in shards:
        draws = jnp.exp(jax.random.uniform(jax.random.fold_in(own, position), (parts,), jnp.float32, least / len(shards), largest / len(shards)))
        factor_of = factor_of * jnp.repeat(draws, dims[position] // parts).reshape([-1 if axis == position else 1 for axis in range(len(dims))])
    return factor_of


def gaussian(rng, dims, width, bound, shards=(), held_as=jnp.bfloat16):
    drawn = width * jax.random.normal(rng, dims, jnp.float32)
    if shards:
        drawn = drawn * block_scale(rng, dims, shards, -0.22, 0.18)
    return jnp.clip(drawn, -bound, bound).astype(held_as)


def setup_inputs(seed: int = 0) -> dict:
    streams_of = jax.random.split(jax.random.key(seed), 9)
    query_stream = gaussian(streams_of[0], (SEGMENTS, SEQ, D), 1.0, 6.0, ((1, 64), (2, 8)))
    key_stream = gaussian(streams_of[1], (SEGMENTS, SEQ, D), 1.0, 6.0, ((1, 64), (2, 8)))
    value_stream = gaussian(streams_of[2], (SEGMENTS, SEQ, D), 1.0, 6.0, ((1, 64), (2, 8)))
    document_starts = touch_ends((jax.random.randint(streams_of[3], (SEGMENTS, SEQ), 0, SEQ // 4) < 1).astype(jnp.int32), jax.random.fold_in(streams_of[3], 1), 0, 1)
    medium_taps = gaussian(streams_of[4], (GROUPS, TAPS), TAPS ** -0.5, 0.5, ((1, 2),))
    modal_rate = jnp.clip(jnp.exp(math.log(0.032958984) - 9.515585 * jax.random.uniform(streams_of[5], (GROUPS, ORDER), jnp.float32) ** block_scale(streams_of[5], (GROUPS, ORDER), ((0, 2), (1, 4)), -0.2, 0.2)), 2.428889274597168e-06, 0.032958984).astype(jnp.bfloat16)
    modal_residue = gaussian(streams_of[6], (GROUPS, ORDER), 1.0, 4.0, ((0, 2), (1, 4)))
    skip_gain = jnp.clip(0.5 + 1.0 * jax.random.uniform(streams_of[7], (D,), jnp.float32) ** block_scale(streams_of[7], (D,), ((0, 8),), -0.2, 0.2), 0.5, 1.5)
    return dict(query_stream=query_stream, key_stream=key_stream, value_stream=value_stream, document_starts=document_starts, medium_taps=medium_taps, modal_rate=modal_rate, modal_residue=modal_residue, skip_gain=skip_gain)


highest = lax.Precision.HIGHEST

def toeplitz_taps(filters, block_len):
    groups = filters.shape[0]
    line = jnp.concatenate([jnp.zeros((groups, 1), filters.dtype), filters[:, ::-1], jnp.zeros((groups, block_len), filters.dtype)], axis=1)
    tiled = jnp.tile(line, (1, block_len))[:, :2 * block_len * block_len]
    return tiled.reshape(groups, block_len, 2 * block_len)

def medium_segment(product, doc_index, medium_taps):
    block_len = TAPS
    block_count = SEQ // block_len
    groups = medium_taps.shape[0]
    channels = product.shape[1] // groups
    matrix = toeplitz_taps(medium_taps.astype(jnp.float32), block_len)
    padded_data = jnp.concatenate([jnp.zeros((block_len, product.shape[1]), jnp.float32), product.astype(jnp.float32)], axis=0)
    padded_docs = jnp.concatenate([jnp.full((block_len,), -1, jnp.int32), doc_index], axis=0)

    def one_block(block_number):
        first_row = block_number * block_len
        window = lax.dynamic_slice_in_dim(padded_data, first_row, 2 * block_len, 0).reshape(2 * block_len, groups, channels)
        window_docs = lax.dynamic_slice_in_dim(padded_docs, first_row, 2 * block_len, 0)
        row_docs = lax.dynamic_slice_in_dim(padded_docs, first_row + block_len, block_len, 0)
        same_doc = row_docs[:, None] == window_docs[None, :]
        masked = jnp.where(same_doc[None], matrix, 0.0)
        result = jnp.einsum('gtj,jgc->tgc', masked, window, precision=highest)
        return result.reshape(block_len, groups * channels)
    outputs = lax.map(one_block, jnp.arange(block_count, dtype=jnp.int32))
    return outputs.reshape(SEQ, groups * channels).astype(jnp.bfloat16)

def modal_blocks(values, doc_index, starts, decay_rate, scaled, carry_state, block_len):
    row_count = values.shape[0]
    block_count = row_count // block_len
    groups = values.shape[1]
    channels = values.shape[2]
    lag_steps = jnp.arange(block_len + 1, dtype=jnp.float32)
    powers = jnp.exp(-decay_rate[:, :, None] * lag_steps)
    kernel = jnp.einsum('gn,gnk->gk', scaled, powers[:, :, :block_len], precision=highest)
    positions = jnp.arange(block_len, dtype=jnp.int32)
    offsets = positions[:, None] - positions[None, :]
    causal = offsets >= 0
    toeplitz = toeplitz_taps(kernel, block_len)[:, :, block_len:]
    carry_weight = scaled[:, None, :] * jnp.transpose(powers[:, :, 1:], (0, 2, 1))
    end_weight = powers[:, :, :block_len][:, :, ::-1]
    full_decay = jnp.transpose(powers[:, :, block_len])

    def advance(state_now, inputs):
        block_values, block_docs, block_starts = inputs
        before = block_docs[0] - block_starts[0]
        continues = block_docs == before
        same_doc = causal & (block_docs[:, None] == block_docs[None, :])
        local_part = jnp.einsum('gts,sgc->tgc', jnp.where(same_doc[None], toeplitz, 0.0), block_values, precision=highest)
        carried = jnp.einsum('gtn,ngc->tgc', jnp.where(continues[None, :, None], carry_weight, 0.0), state_now, precision=highest)
        keep_mask = block_docs == block_docs[block_len - 1]
        emitted = jnp.einsum('gns,sgc->ngc', jnp.where(keep_mask[None, None, :], end_weight, 0.0), block_values, precision=highest)
        factor = jnp.where(continues[block_len - 1], full_decay, 0.0)
        return (factor[:, :, None] * state_now + emitted, local_part + carried)
    final_state, outputs = lax.scan(advance, carry_state, (values.reshape(block_count, block_len, groups, channels), doc_index.reshape(block_count, block_len), starts.reshape(block_count, block_len)))
    return (outputs.reshape(row_count, groups, channels), final_state)

def reference(query_stream, key_stream, value_stream, document_starts, medium_taps, modal_rate, modal_residue, skip_gain):
    decay_rate = modal_rate.astype(jnp.float32)
    mode_count = decay_rate.shape[1]
    scaled = modal_residue.astype(jnp.float32) * jnp.sqrt((1.0 - jnp.exp(-2.0 * decay_rate)) / mode_count)
    results = []
    for segment in range(SEGMENTS):
        product = (key_stream[segment].astype(jnp.float32) * value_stream[segment].astype(jnp.float32)).astype(jnp.bfloat16)
        starts = document_starts[segment].astype(jnp.int32)
        doc_index = jnp.cumsum(starts).astype(jnp.int32)
        medium = medium_segment(product, doc_index, medium_taps)
        gated_values = (query_stream[segment].astype(jnp.float32) * medium.astype(jnp.float32)).astype(jnp.bfloat16)
        values = gated_values.astype(jnp.float32).reshape(SEQ, GROUPS, GROUP_CH)
        zero_state = jnp.zeros((mode_count, GROUPS, GROUP_CH), jnp.float32)
        long_part, final_state = modal_blocks(values, doc_index, starts, decay_rate, scaled, zero_state, TAPS)
        combined = long_part.reshape(SEQ, D) + skip_gain[None, :] * gated_values.astype(jnp.float32)
        results.append(combined.astype(jnp.bfloat16))
    return jnp.stack(results)
```

```python
import functools

import jax
import jax.numpy as jnp
from jax import lax
from jax.experimental import pallas as pl
from jax.experimental.pallas import tpu as pltpu
from jax.sharding import PartitionSpec as P

MESH = pl.DeviceIdType.MESH
CH = 16
MODES = 16
TOK = 128
LANES = 256
GB = LANES // CH
NB = 4
WIDE = NB * LANES
GROUPS = WIDE // CH
CTX = 64

f32 = jnp.float32
bf16 = jnp.bfloat16


def iota(shape, dim):
    return lax.broadcasted_iota(jnp.int32, shape, dim)


def one_hot(cond):
    return jnp.where(cond, 1.0, 0.0).astype(bf16)


def dot(a, b):
    return jnp.dot(a, b, preferred_element_type=f32)


def minus_expm1_neg(x):
    series = x * (1.0 - x * (0.5 - x * (1.0 / 6 - x * (1.0 / 24 - x * (1.0 / 120 - x * (1.0 / 720))))))
    return jnp.where(x < 0.125, series, 1.0 - jnp.exp(-x))


def scaled_of(rate, residue):
    return residue * jnp.sqrt(minus_expm1_neg(2.0 * rate) * (1.0 / MODES))


def kernel(
    q_hbm, k_hbm, v_hbm, starts, taps_hbm, rate_hbm, residue_hbm, skip, out,
    q_buf, k_buf, v_buf, window, tapbuf, ratebuf, resbuf, line, hline, toep, modal, ends, carry,
    gated, partial, e_buf, recv, prefix, states,
    in_sem, halo_send, halo_recv, tap_send, tap_recv, mod_send, mod_recv, p1_send, p1_recv, p2_send, p2_recv,
):
    fs = lax.axis_index("fsdp")
    cx = lax.axis_index("ctx")
    dp = lax.axis_index("dp")

    loads = [
        pltpu.make_async_copy(k_hbm.at[0], k_buf, in_sem.at[0]),
        pltpu.make_async_copy(v_hbm.at[0], v_buf, in_sem.at[1]),
        pltpu.make_async_copy(q_hbm.at[0], q_buf, in_sem.at[2]),
    ]
    for load in loads:
        load.start()

    barrier = pltpu.get_barrier_semaphore()

    def greet(d, c):
        pl.semaphore_signal(
            barrier, inc=1, device_id=(fs, lax.rem(cx + d, CTX), dp), device_id_type=MESH
        )
        return c

    lax.fori_loop(1, CTX, greet, 0)
    pl.semaphore_signal(barrier, inc=1, device_id=(1 - fs, cx, dp), device_id_type=MESH)
    for d in (1, 2, 3):
        pl.semaphore_signal(
            barrier, inc=1, device_id=(fs, cx, lax.rem(dp + d, 4)), device_id_type=MESH
        )

    own_row = starts[pl.ds(cx, 1), :].astype(f32)
    before_row = starts[pl.ds(lax.rem(cx + CTX - 1, CTX), 1), :].astype(f32)
    both = jnp.concatenate([before_row, own_row], axis=1)
    t_of = iota((TOK, 2 * TOK), 0)
    s_of = iota((TOK, 2 * TOK), 1)
    at_row = jnp.sum(jnp.where(s_of <= t_of + TOK, both, 0.0), axis=1, keepdims=True)
    upper = one_hot(iota((2 * TOK, 2 * TOK), 0) <= iota((2 * TOK, 2 * TOK), 1))
    counts = dot(jnp.broadcast_to(both, (8, 2 * TOK)).astype(bf16), upper)[0:1]
    first = jnp.where(cx == 0, TOK, 0)
    mask = jnp.where((at_row == counts) & (s_of <= t_of + TOK) & (s_of >= first), 1.0, 0.0)
    before = jnp.sum(before_row, axis=1, keepdims=True)
    total = before + jnp.sum(own_row, axis=1, keepdims=True)
    keep = jnp.where(counts[:, TOK:] == total, 1.0, 0.0)
    continues = jnp.where(at_row == before, 1.0, 0.0)

    loads[0].wait()
    loads[1].wait()
    for j in range(NB):
        cols = pl.ds(j * LANES, LANES)
        window[j, TOK:, :] = (k_buf[:, cols].astype(f32) * v_buf[:, cols].astype(f32)).astype(bf16)

    @pl.when(cx == 0)
    def _():
        for j in range(NB):
            window[j, :TOK, :] = jnp.zeros((TOK, LANES), bf16)

    pl.semaphore_wait(barrier, CTX - 1 + 4)

    halos = [
        pltpu.make_async_remote_copy(
            window.at[j, pl.ds(TOK, TOK)], window.at[j, pl.ds(0, TOK)], halo_send.at[j], halo_recv.at[j],
            device_id=(fs, lax.rem(cx + 1, CTX), dp), device_id_type=MESH,
        )
        for j in range(NB)
    ]

    @pl.when(cx < CTX - 1)
    def _():
        for halo in halos:
            halo.start()

    other = pl.multiple_of(((1 - fs) * 4 + dp) * GROUPS, GROUPS)
    mine = pl.multiple_of((fs * 4 + dp) * GROUPS, GROUPS)
    tap_copy = pltpu.make_async_remote_copy(
        taps_hbm.at[pl.ds(other, GROUPS)], tapbuf.at[fs], tap_send, tap_recv,
        device_id=(1 - fs, cx, dp), device_id_type=MESH,
    )
    tap_copy.start()
    tap_own = pltpu.make_async_copy(taps_hbm.at[pl.ds(mine, GROUPS)], tapbuf.at[fs], in_sem.at[3])
    tap_own.start()
    modal_copies = []
    for d in (1, 2, 3):
        to = lax.rem(dp + d, 4)
        rows = pl.ds(pl.multiple_of(to * GROUPS, GROUPS), GROUPS)
        for i, (src, dst) in enumerate(((rate_hbm, ratebuf), (residue_hbm, resbuf))):
            copy = pltpu.make_async_remote_copy(
                src.at[rows], dst.at[dp], mod_send.at[i, d - 1], mod_recv.at[i, d - 1],
                device_id=(fs, cx, to), device_id_type=MESH,
            )
            copy.start()
            modal_copies.append(copy)
    rows = pl.ds(pl.multiple_of(dp * GROUPS, GROUPS), GROUPS)
    rate_own = pltpu.make_async_copy(rate_hbm.at[rows], ratebuf.at[dp], in_sem.at[4])
    residue_own = pltpu.make_async_copy(residue_hbm.at[rows], resbuf.at[dp], in_sem.at[5])
    rate_own.start()
    residue_own.start()

    tap_own.wait()
    tap_copy.wait()
    flip = [one_hot(iota((TOK // 2, 2 * TOK), 1) == TOK - h * (TOK // 2) - iota((TOK // 2, 2 * TOK), 0)) for h in (0, 1)]
    line[...] = dot(tapbuf[0], flip[0]) + dot(tapbuf[1], flip[1])

    def build_medium(g, c):
        row = jnp.broadcast_to(line[pl.ds(g, 1), :], (TOK, 2 * TOK))
        toep[g] = (pltpu.roll(row, 0, 1, stride=1, stride_axis=0) * mask).astype(bf16)
        return c

    lax.fori_loop(0, GROUPS, build_medium, 0)

    rate_own.wait()
    residue_own.wait()
    for copy in modal_copies:
        copy.wait()

    def gather_modes(buf):
        parts = [dot(buf[d], one_hot(iota((4, MODES), 1) == 4 * d + iota((4, MODES), 0))) for d in range(4)]
        return (parts[0] + parts[1]) + (parts[2] + parts[3])

    rate16 = gather_modes(ratebuf)
    res16 = gather_modes(resbuf)
    repeat = one_hot(iota((GROUPS * MODES, GROUPS), 0) // MODES == iota((GROUPS * MODES, GROUPS), 1))
    own_mode = iota((GROUPS * MODES, MODES), 0) % MODES == iota((GROUPS * MODES, MODES), 1)
    ones = jnp.ones((MODES, TOK), bf16)

    def column(per_group):
        spread = jnp.where(own_mode, dot(repeat, per_group.astype(bf16)), 0.0)
        return dot(spread.astype(bf16), ones)

    rate_col = column(rate16)
    scaled_col = scaled_of(rate_col, column(res16))
    lag = ((TOK - iota((1, TOK), 1)) % TOK).astype(f32)
    powers = jnp.exp(-rate_col * lag)
    hline[...] = jnp.sum((powers * scaled_col).reshape(GROUPS, MODES, TOK), axis=1)
    ends[...] = (pltpu.roll(powers, TOK - 1, 1) * keep).astype(bf16)

    def build_modal(g, c):
        row = jnp.broadcast_to(hline[pl.ds(g, 1), :], (TOK, TOK))
        modal[g] = (pltpu.roll(row, 0, 1, stride=1, stride_axis=0) * mask[:, TOK:]).astype(bf16)
        return c

    lax.fori_loop(0, GROUPS, build_modal, 0)

    tile = one_hot(iota((MODES, GROUPS * MODES), 1) % MODES == iota((MODES, GROUPS * MODES), 0))
    own_group = iota((GROUPS, GROUPS * MODES), 1) // MODES == iota((GROUPS, GROUPS * MODES), 0)

    def as_row(per_group):
        spread = jnp.where(own_group, dot(per_group.astype(bf16), tile), 0.0)
        return jnp.sum(spread, axis=0, keepdims=True)

    rate_row = as_row(rate16)
    scaled_row = scaled_of(rate_row, as_row(res16))
    steps = (iota((TOK, 1), 0) + 1).astype(f32)
    carry[...] = (jnp.exp(-rate_row * steps) * scaled_row * continues).astype(bf16)

    med_mode = lax.rem(cx, MODES)
    med_block = cx // MODES
    rate_mode = jnp.sum(jnp.where(iota((GROUPS, MODES), 1) == med_mode, rate16, 0.0), axis=1, keepdims=True)
    group_of = med_block * GB + iota((GROUPS, LANES), 1) // CH
    rate_med = jnp.sum(jnp.where(group_of == iota((GROUPS, LANES), 0), rate_mode, 0.0), axis=0, keepdims=True)
    no_start = jnp.where(jnp.sum(starts[...], axis=1, keepdims=True) == 0, 1.0, 0.0)
    a = jnp.exp(-rate_med * TOK) * no_start
    place = iota((CTX, 1), 0)
    scales = []
    for step in (1, 2, 4, 8, 16, 32):
        a = jnp.where(place >= step, a, 0.0)
        scales.append(a)
        a = a * pltpu.roll(a, step, 0)

    loads[2].wait()
    lane_group = iota((1, LANES), 1) // CH

    for j in range(NB):
        @pl.when(cx > 0)
        def _():
            halos[j].wait_recv()

        data = window[j]
        groups = [dot(toep[j * GB + i], data) for i in range(GB)]
        medium = groups[0]
        for i in range(1, GB):
            medium = jnp.where(lane_group == i, groups[i], medium)
        value = (q_buf[:, j * LANES:(j + 1) * LANES].astype(f32) * medium.astype(bf16).astype(f32)).astype(bf16)
        gated[j] = value
        full = dot(ends[pl.ds(j * GB * MODES, GB * MODES), :], value)
        state = full[0:MODES]
        for i in range(1, GB):
            state = jnp.where(lane_group == i, full[i * MODES:(i + 1) * MODES], state)
        e_buf[j] = state

        def send_one(n, c):
            to = j * MODES + n

            @pl.when(to != cx)
            def _():
                pltpu.make_async_remote_copy(
                    e_buf.at[j, pl.ds(n, 1)], recv.at[pl.ds(cx, 1)], p1_send, p1_recv,
                    device_id=(fs, to, dp), device_id_type=MESH,
                ).start()

            @pl.when(to == cx)
            def _():
                pltpu.make_async_copy(e_buf.at[j, pl.ds(n, 1)], recv.at[pl.ds(cx, 1)], p1_recv).start()

            return c

        lax.fori_loop(0, MODES, send_one, 0)

    for j in range(NB):
        value = gated[j]
        groups = [dot(modal[j * GB + i], value) for i in range(GB)]
        inside = groups[0]
        for i in range(1, GB):
            inside = jnp.where(lane_group == i, groups[i], inside)
        partial[j] = inside + skip[:, j * LANES:(j + 1) * LANES] * value.astype(f32)

    pltpu.make_async_copy(recv, recv, p1_recv).wait()
    b = recv[...]
    for step, scale in zip((1, 2, 4, 8, 16, 32), scales):
        b = b + scale * pltpu.roll(b, step, 0)
    prefix[...] = jnp.where(place == 0, 0.0, pltpu.roll(b, 1, 0))

    def return_one(d, c):
        to = lax.rem(cx + d, CTX)
        pltpu.make_async_remote_copy(
            prefix.at[pl.ds(to, 1)], states.at[med_block, pl.ds(med_mode, 1)], p2_send, p2_recv.at[med_block],
            device_id=(fs, to, dp), device_id_type=MESH,
        ).start()
        return c

    pltpu.make_async_copy(prefix.at[pl.ds(cx, 1)], states.at[med_block, pl.ds(med_mode, 1)], p2_recv.at[med_block]).start()
    lax.fori_loop(1, CTX, return_one, 0)

    diagonal = iota((LANES, LANES), 0) // MODES == iota((LANES, LANES), 1) // CH
    for j in range(NB):
        pltpu.make_async_copy(states.at[j], states.at[j], p2_recv.at[j]).wait()
        spread = jnp.where(diagonal, jnp.concatenate([states[j]] * GB, axis=0), 0.0).astype(bf16)
        carried = dot(carry[:, j * LANES:(j + 1) * LANES], spread)
        out[0, :, j * LANES:(j + 1) * LANES] = (partial[j] + carried).astype(bf16)

    @pl.when(cx < CTX - 1)
    def _():
        for halo in halos:
            halo.wait_send()

    for sem in (p1_send, p2_send):
        pltpu.make_async_copy(prefix.at[pl.ds(0, 56)], prefix.at[pl.ds(0, 56)], sem).wait()

        def drain(i, c):
            pltpu.make_async_copy(prefix.at[pl.ds(i, 1)], prefix.at[pl.ds(i, 1)], sem).wait()
            return c

        lax.fori_loop(0, 7, drain, 0)


def body(query, key, value, starts, taps, rate, residue, skip):
    any_space = pl.BlockSpec(memory_space=pl.ANY)
    vmem = pl.BlockSpec(memory_space=pltpu.VMEM)
    dma = pltpu.SemaphoreType.DMA
    return pl.pallas_call(
        kernel,
        out_shape=jax.ShapeDtypeStruct((1, TOK, WIDE), bf16),
        in_specs=[any_space] * 3 + [vmem] + [any_space] * 3 + [vmem],
        out_specs=vmem,
        scratch_shapes=[
            pltpu.VMEM((TOK, WIDE), bf16),
            pltpu.VMEM((TOK, WIDE), bf16),
            pltpu.VMEM((TOK, WIDE), bf16),
            pltpu.VMEM((NB, 2 * TOK, LANES), bf16),
            pltpu.VMEM((2, GROUPS, TOK // 2), bf16),
            pltpu.VMEM((4, GROUPS, 4), bf16),
            pltpu.VMEM((4, GROUPS, 4), bf16),
            pltpu.VMEM((GROUPS, 2 * TOK), f32),
            pltpu.VMEM((GROUPS, TOK), f32),
            pltpu.VMEM((GROUPS, TOK, 2 * TOK), bf16),
            pltpu.VMEM((GROUPS, TOK, TOK), bf16),
            pltpu.VMEM((GROUPS * MODES, TOK), bf16),
            pltpu.VMEM((TOK, GROUPS * MODES), bf16),
            pltpu.VMEM((NB, TOK, LANES), bf16),
            pltpu.VMEM((NB, TOK, LANES), f32),
            pltpu.VMEM((NB, MODES, LANES), f32),
            pltpu.VMEM((CTX, LANES), f32),
            pltpu.VMEM((CTX, LANES), f32),
            pltpu.VMEM((NB, MODES, LANES), f32),
            dma((6,)), dma((NB,)), dma((NB,)), dma, dma, dma((2, 3)), dma((2, 3)),
            dma, dma, dma, dma((NB,)),
        ],
        compiler_params=pltpu.CompilerParams(
            collective_id=1, has_side_effects=True, vmem_limit_bytes=48 * 1024 * 1024
        ),
    )(query, key, value, starts.reshape(CTX, TOK), taps, rate, residue, skip.reshape(1, WIDE))


def solution(mesh):
    return jax.shard_map(
        body,
        mesh=mesh,
        in_specs=(
            P(None, "ctx", ("fsdp", "dp")),
            P(None, "ctx", ("fsdp", "dp")),
            P(None, "ctx", ("fsdp", "dp")),
            P(),
            P(None, "fsdp"),
            P("fsdp", "dp"),
            P("fsdp", "dp"),
            P(("fsdp", "dp")),
        ),
        out_specs=P(None, "ctx", ("fsdp", "dp")),
        check_vma=False,
    )
```

```python
import functools

import jax
import jax.numpy as jnp
from jax import lax
from jax.experimental import pallas as pl
from jax.experimental.pallas import tpu as pltpu
from jax.sharding import PartitionSpec as P

MESH = pl.DeviceIdType.MESH
CH = 16
MODES = 16
TOK = 128
LANES = 256
GB = LANES // CH
NB = 4
WIDE = NB * LANES
GROUPS = WIDE // CH
PAIR = 2 * GROUPS
CTX = 64
STRIP = 16
STRIPS = TOK // STRIP

f32 = jnp.float32
bf16 = jnp.bfloat16


def iota(shape, dim):
    return lax.broadcasted_iota(jnp.int32, shape, dim)


def one_hot(cond):
    return jnp.where(cond, 1.0, 0.0).astype(bf16)


def dot(a, b):
    return jnp.dot(a, b, preferred_element_type=f32)


def dot_rows(a, b):
    return lax.dot_general(a, b, (((0,), (0,)), ((), ())), preferred_element_type=f32)


def minus_expm1_neg(x):
    series = x * (1.0 - x * (0.5 - x * (1.0 / 6 - x * (1.0 / 24 - x * (1.0 / 120 - x * (1.0 / 720))))))
    return jnp.where(x < 0.125, series, 1.0 - jnp.exp(-x))


def scaled_of(rate, residue):
    return residue * jnp.sqrt(minus_expm1_neg(2.0 * rate) * (1.0 / MODES))


def kernel(
    q_hbm, k_hbm, v_hbm, starts, taps_hbm, rate_hbm, residue_hbm, skip, out,
    q_buf, k_buf, v_buf, window, tapbuf, ratebuf, resbuf, line, hline, toep, modal, ends, carry,
    gated, partial, e_buf, recv, prefix, states,
    in_sem, halo_send, halo_recv, tap_send, tap_recv, mod_send, mod_recv, p1_send, p1_recv, p2_send, p2_recv,
):
    fs = lax.axis_index("fsdp")
    cx = lax.axis_index("ctx")
    dp = lax.axis_index("dp")

    loads = [
        pltpu.make_async_copy(k_hbm.at[0], k_buf, in_sem.at[0]),
        pltpu.make_async_copy(v_hbm.at[0], v_buf, in_sem.at[1]),
        pltpu.make_async_copy(q_hbm.at[0], q_buf, in_sem.at[2]),
    ]
    for load in loads:
        load.start()

    barrier = pltpu.get_barrier_semaphore()

    def greet(d, c):
        pl.semaphore_signal(
            barrier, inc=1, device_id=(fs, lax.rem(cx + d, CTX), dp), device_id_type=MESH
        )
        return c

    lax.fori_loop(1, CTX, greet, 0)
    pl.semaphore_signal(barrier, inc=1, device_id=(1 - fs, cx, dp), device_id_type=MESH)
    for d in (1, 2, 3):
        pl.semaphore_signal(
            barrier, inc=1, device_id=(fs, cx, lax.rem(dp + d, 4)), device_id_type=MESH
        )

    own_row = starts[pl.ds(cx, 1), :].astype(f32)
    before_row = starts[pl.ds(lax.rem(cx + CTX - 1, CTX), 1), :].astype(f32)
    both = jnp.concatenate([before_row, own_row], axis=1)
    t_of = iota((TOK, 2 * TOK), 0)
    s_of = iota((TOK, 2 * TOK), 1)
    at_row = jnp.sum(jnp.where(s_of <= t_of + TOK, both, 0.0), axis=1, keepdims=True)
    upper = one_hot(iota((2 * TOK, 2 * TOK), 0) <= iota((2 * TOK, 2 * TOK), 1))
    counts = dot(jnp.broadcast_to(both, (8, 2 * TOK)).astype(bf16), upper)[0:1]
    first = jnp.where(cx == 0, TOK, 0)
    mask = jnp.where((at_row == counts) & (s_of <= t_of + TOK) & (s_of >= first), 1.0, 0.0)
    before = jnp.sum(before_row, axis=1, keepdims=True)
    total = before + jnp.sum(own_row, axis=1, keepdims=True)
    keep = jnp.where(counts[:, TOK:] == total, 1.0, 0.0)
    continues = jnp.where(at_row == before, 1.0, 0.0)

    loads[0].wait()
    loads[1].wait()
    for j in range(NB):
        cols = pl.ds(j * LANES, LANES)
        window[j, TOK:2 * TOK, :] = (k_buf[:, cols].astype(f32) * v_buf[:, cols].astype(f32)).astype(bf16)
        window[j, 2 * TOK:, :] = jnp.zeros((TOK, LANES), bf16)
        gated[j, :TOK - STRIP, :] = jnp.zeros((TOK - STRIP, LANES), bf16)

    @pl.when(cx == 0)
    def _():
        for j in range(NB):
            window[j, :TOK, :] = jnp.zeros((TOK, LANES), bf16)

    pl.semaphore_wait(barrier, CTX - 1 + 4)

    halos = [
        pltpu.make_async_remote_copy(
            window.at[j, pl.ds(TOK, TOK)], window.at[j, pl.ds(0, TOK)], halo_send.at[j], halo_recv.at[j],
            device_id=(fs, lax.rem(cx + 1, CTX), dp), device_id_type=MESH,
        )
        for j in range(NB)
    ]

    @pl.when(cx < CTX - 1)
    def _():
        for halo in halos:
            halo.start()

    half = lax.rem(dp, 2) * GROUPS
    other = pl.multiple_of(((1 - fs) * 2 + dp // 2) * PAIR, PAIR)
    mine = pl.multiple_of((fs * 2 + dp // 2) * PAIR, PAIR)
    tap_copy = pltpu.make_async_remote_copy(
        taps_hbm.at[:, pl.ds(other, PAIR)], tapbuf.at[fs], tap_send, tap_recv,
        device_id=(1 - fs, cx, dp), device_id_type=MESH,
    )
    tap_copy.start()
    tap_own = pltpu.make_async_copy(taps_hbm.at[:, pl.ds(mine, PAIR)], tapbuf.at[fs], in_sem.at[3])
    tap_own.start()
    modal_copies = []
    for d in (1, 2, 3):
        to = lax.rem(dp + d, 4)
        pair = pl.ds(pl.multiple_of(to // 2 * PAIR, PAIR), PAIR)
        for i, (src, dst) in enumerate(((rate_hbm, ratebuf), (residue_hbm, resbuf))):
            copy = pltpu.make_async_remote_copy(
                src.at[:, pair], dst.at[dp], mod_send.at[i, d - 1], mod_recv.at[i, d - 1],
                device_id=(fs, cx, to), device_id_type=MESH,
            )
            copy.start()
            modal_copies.append(copy)
    pair = pl.ds(pl.multiple_of(dp // 2 * PAIR, PAIR), PAIR)
    rate_own = pltpu.make_async_copy(rate_hbm.at[:, pair], ratebuf.at[dp], in_sem.at[4])
    residue_own = pltpu.make_async_copy(residue_hbm.at[:, pair], resbuf.at[dp], in_sem.at[5])
    rate_own.start()
    residue_own.start()

    tap_own.wait()
    tap_copy.wait()
    flip = [one_hot(iota((TOK // 2, 2 * TOK), 1) == TOK - h * (TOK // 2) - iota((TOK // 2, 2 * TOK), 0)) for h in (0, 1)]
    line[...] = dot_rows(tapbuf[0], flip[0]) + dot_rows(tapbuf[1], flip[1])

    wide_lane = iota((STRIP, 2 * TOK), 1)
    wide_masks = []
    for a in range(STRIPS):
        part = mask[a * STRIP:(a + 1) * STRIP]
        if a:
            part = pltpu.roll(part, 2 * TOK - a * STRIP, 1)
        wide_masks.append(jnp.where(wide_lane < TOK + STRIP, part, 0.0).astype(bf16))

    def build_medium(g, c):
        row = jnp.broadcast_to(line[pl.ds(half + g, 1), :], (STRIP, 2 * TOK))
        base = pltpu.roll(row, 0, 1, stride=1, stride_axis=0).astype(bf16)
        at = pl.ds(pl.multiple_of((g & 15) * STRIP, STRIP), STRIP)
        for a in range(STRIPS):
            toep[(g >> 4) * STRIPS + a, at, :] = base * wide_masks[a]
        return c

    lax.fori_loop(0, GROUPS, build_medium, 0, unroll=8)

    rate_own.wait()
    residue_own.wait()
    for copy in modal_copies:
        copy.wait()

    def gather_modes(buf):
        parts = [dot_rows(buf[d], one_hot(iota((4, MODES), 1) == 4 * d + iota((4, MODES), 0))) for d in range(4)]
        return (parts[0] + parts[1]) + (parts[2] + parts[3])

    rate16 = gather_modes(ratebuf)
    res16 = gather_modes(resbuf)
    repeat = one_hot(half + (iota((GROUPS * MODES, PAIR), 0) >> 4) == iota((GROUPS * MODES, PAIR), 1))
    own_mode = (iota((GROUPS * MODES, MODES), 0) & 15) == iota((GROUPS * MODES, MODES), 1)
    ones = jnp.ones((MODES, TOK), bf16)

    def column(per_group):
        spread = jnp.where(own_mode, dot(repeat, per_group.astype(bf16)), 0.0)
        return dot(spread.astype(bf16), ones)

    rate_col = column(rate16)
    scaled_col = scaled_of(rate_col, column(res16))
    lag = ((TOK - STRIP - iota((1, TOK), 1)) & (TOK - 1)).astype(f32)
    powers = jnp.exp(-rate_col * lag)
    hline[...] = jnp.sum((powers * scaled_col).reshape(GROUPS, MODES, TOK), axis=1)
    ends[...] = (pltpu.roll(powers, STRIP - 1, 1) * keep).astype(bf16)

    lane = iota((STRIP, TOK), 1)
    masks = []
    for a in range(STRIPS):
        part = mask[a * STRIP:(a + 1) * STRIP, TOK:]
        shift = TOK - STRIP - a * STRIP
        if shift:
            part = jnp.where(lane >= shift, pltpu.roll(part, shift, 1), 0.0)
        masks.append(part.astype(bf16))

    def build_modal(g, c):
        row = jnp.broadcast_to(hline[pl.ds(g, 1), :], (STRIP, TOK))
        base = pltpu.roll(row, 0, 1, stride=1, stride_axis=0).astype(bf16)
        at = pl.ds(pl.multiple_of((g & 15) * STRIP, STRIP), STRIP)
        for a in range(STRIPS):
            modal[(g >> 4) * STRIPS + a, at, :] = base * masks[a]
        return c

    lax.fori_loop(0, GROUPS, build_modal, 0, unroll=8)

    tile = one_hot((iota((MODES, GROUPS * MODES), 1) & 15) == iota((MODES, GROUPS * MODES), 0))
    own_group = half + (iota((PAIR, GROUPS * MODES), 1) >> 4) == iota((PAIR, GROUPS * MODES), 0)

    def as_row(per_group):
        spread = jnp.where(own_group, dot(per_group.astype(bf16), tile), 0.0)
        return jnp.sum(spread, axis=0, keepdims=True)

    rate_row = as_row(rate16)
    scaled_row = scaled_of(rate_row, as_row(res16))
    steps = (iota((TOK, 1), 0) + 1).astype(f32)
    carry[...] = (jnp.exp(-rate_row * steps) * scaled_row * continues).astype(bf16)

    med_mode = lax.rem(cx, MODES)
    med_block = cx // MODES
    rate_mode = jnp.sum(jnp.where(iota((PAIR, MODES), 1) == med_mode, rate16, 0.0), axis=1, keepdims=True)
    group_of = half + med_block * GB + (iota((PAIR, LANES), 1) >> 4)
    rate_med = jnp.sum(jnp.where(group_of == iota((PAIR, LANES), 0), rate_mode, 0.0), axis=0, keepdims=True)
    no_start = jnp.where(jnp.sum(starts[...], axis=1, keepdims=True) == 0, 1.0, 0.0)
    a = jnp.exp(-rate_med * TOK) * no_start
    place = iota((CTX, 1), 0)
    scales = []
    for step in (1, 2, 4, 8, 16, 32):
        a = jnp.where(place >= step, a, 0.0)
        scales.append(a)
        a = a * pltpu.roll(a, step, 0)

    loads[2].wait()
    lane_group = iota((1, LANES), 1) >> 4

    def pick(rows, size):
        out_rows = rows[:size]
        for i in range(1, GB):
            out_rows = jnp.where(lane_group == i, rows[i * size:(i + 1) * size], out_rows)
        return out_rows

    for j in range(NB):
        @pl.when(cx > 0)
        def _():
            halos[j].wait_recv()

        medium = jnp.concatenate(
            [pick(dot(toep[j * STRIPS + a], window[j, a * STRIP:a * STRIP + 2 * TOK, :]), STRIP) for a in range(STRIPS)], axis=0
        )
        value = (q_buf[:, j * LANES:(j + 1) * LANES].astype(f32) * medium.astype(bf16).astype(f32)).astype(bf16)
        gated[j, TOK - STRIP:, :] = value
        full = dot(ends[pl.ds(j * GB * MODES, GB * MODES), :], value)
        e_buf[j] = pick(full, MODES)

        def send_one(n, c):
            to = j * MODES + n

            @pl.when(to != cx)
            def _():
                pltpu.make_async_remote_copy(
                    e_buf.at[j, pl.ds(n, 1)], recv.at[pl.ds(cx, 1)], p1_send, p1_recv,
                    device_id=(fs, to, dp), device_id_type=MESH,
                ).start()

            @pl.when(to == cx)
            def _():
                pltpu.make_async_copy(e_buf.at[j, pl.ds(n, 1)], recv.at[pl.ds(cx, 1)], p1_recv).start()

            return c

        lax.fori_loop(0, MODES, send_one, 0)

    for j in range(NB):
        value = gated[j, TOK - STRIP:, :]
        inside = jnp.concatenate(
            [pick(dot(modal[j * STRIPS + a], gated[j, a * STRIP:a * STRIP + TOK, :]), STRIP) for a in range(STRIPS)], axis=0
        )
        partial[j] = inside + skip[:, j * LANES:(j + 1) * LANES] * value.astype(f32)

    pltpu.make_async_copy(recv, recv, p1_recv).wait()
    b = recv[...]
    for step, scale in zip((1, 2, 4, 8, 16, 32), scales):
        b = b + scale * pltpu.roll(b, step, 0)
    prefix[...] = jnp.where(place == 0, 0.0, pltpu.roll(b, 1, 0))

    def return_one(d, c):
        to = lax.rem(cx + d, CTX)
        pltpu.make_async_remote_copy(
            prefix.at[pl.ds(to, 1)], states.at[med_block, pl.ds(med_mode, 1)], p2_send, p2_recv.at[med_block],
            device_id=(fs, to, dp), device_id_type=MESH,
        ).start()
        return c

    pltpu.make_async_copy(prefix.at[pl.ds(cx, 1)], states.at[med_block, pl.ds(med_mode, 1)], p2_recv.at[med_block]).start()
    lax.fori_loop(1, CTX, return_one, 0)

    diagonal = (iota((LANES, LANES), 0) >> 4) == (iota((LANES, LANES), 1) >> 4)
    for j in range(NB):
        pltpu.make_async_copy(states.at[j], states.at[j], p2_recv.at[j]).wait()
        spread = jnp.where(diagonal, jnp.concatenate([states[j]] * GB, axis=0), 0.0).astype(bf16)
        carried = dot(carry[:, j * LANES:(j + 1) * LANES], spread)
        out[0, :, j * LANES:(j + 1) * LANES] = (partial[j] + carried).astype(bf16)

    @pl.when(cx < CTX - 1)
    def _():
        for halo in halos:
            halo.wait_send()

    for sem in (p1_send, p2_send):
        pltpu.make_async_copy(prefix.at[pl.ds(0, 56)], prefix.at[pl.ds(0, 56)], sem).wait()

        def drain(i, c):
            pltpu.make_async_copy(prefix.at[pl.ds(i, 1)], prefix.at[pl.ds(i, 1)], sem).wait()
            return c

        lax.fori_loop(0, 7, drain, 0)


def body(query, key, value, starts, taps, rate, residue, skip):
    any_space = pl.BlockSpec(memory_space=pl.ANY)
    vmem = pl.BlockSpec(memory_space=pltpu.VMEM)
    dma = pltpu.SemaphoreType.DMA
    return pl.pallas_call(
        kernel,
        out_shape=jax.ShapeDtypeStruct((1, TOK, WIDE), bf16),
        in_specs=[any_space] * 3 + [vmem] + [any_space] * 3 + [vmem],
        out_specs=vmem,
        scratch_shapes=[
            pltpu.VMEM((TOK, WIDE), bf16),
            pltpu.VMEM((TOK, WIDE), bf16),
            pltpu.VMEM((TOK, WIDE), bf16),
            pltpu.VMEM((NB, 3 * TOK, LANES), bf16),
            pltpu.VMEM((2, TOK // 2, PAIR), bf16),
            pltpu.VMEM((4, 4, PAIR), bf16),
            pltpu.VMEM((4, 4, PAIR), bf16),
            pltpu.VMEM((PAIR, 2 * TOK), f32),
            pltpu.VMEM((GROUPS, TOK), f32),
            pltpu.VMEM((NB * STRIPS, GB * STRIP, 2 * TOK), bf16),
            pltpu.VMEM((NB * STRIPS, GB * STRIP, TOK), bf16),
            pltpu.VMEM((GROUPS * MODES, TOK), bf16),
            pltpu.VMEM((TOK, GROUPS * MODES), bf16),
            pltpu.VMEM((NB, 2 * TOK - STRIP, LANES), bf16),
            pltpu.VMEM((NB, TOK, LANES), f32),
            pltpu.VMEM((NB, MODES, LANES), f32),
            pltpu.VMEM((CTX, LANES), f32),
            pltpu.VMEM((CTX, LANES), f32),
            pltpu.VMEM((NB, MODES, LANES), f32),
            dma((6,)), dma((NB,)), dma((NB,)), dma, dma, dma((2, 3)), dma((2, 3)),
            dma, dma, dma, dma((NB,)),
        ],
        compiler_params=pltpu.CompilerParams(
            collective_id=1, has_side_effects=True, vmem_limit_bytes=67_043_328
        ),
    )(query, key, value, starts.reshape(CTX, TOK), taps.T, rate.T, residue.T, skip.reshape(1, WIDE))


def solution(mesh):
    return jax.shard_map(
        body,
        mesh=mesh,
        in_specs=(
            P(None, "ctx", ("fsdp", "dp")),
            P(None, "ctx", ("fsdp", "dp")),
            P(None, "ctx", ("fsdp", "dp")),
            P(),
            P(None, "fsdp"),
            P("fsdp", "dp"),
            P("fsdp", "dp"),
            P(("fsdp", "dp")),
        ),
        out_specs=P(None, "ctx", ("fsdp", "dp")),
        check_vma=False,
    )
```

```python
import functools

import jax
import jax.numpy as jnp
from jax import lax
from jax.experimental import pallas as pl
from jax.experimental.pallas import tpu as pltpu
from jax.sharding import PartitionSpec as P

MESH = pl.DeviceIdType.MESH
CH = 16
MODES = 16
TOK = 128
LANES = 256
GB = LANES // CH
NB = 4
WIDE = NB * LANES
GROUPS = WIDE // CH
PAIR = 2 * GROUPS
CTX = 64
ROW = 16
STRIP = 16
STRIPS = TOK // STRIP

f32 = jnp.float32
bf16 = jnp.bfloat16


def iota(shape, dim):
    return lax.broadcasted_iota(jnp.int32, shape, dim)


def one_hot(cond):
    return jnp.where(cond, 1.0, 0.0).astype(bf16)


def dot(a, b):
    return jnp.dot(a, b, preferred_element_type=f32)


def dot_rows(a, b):
    return lax.dot_general(a, b, (((0,), (0,)), ((), ())), preferred_element_type=f32)


def minus_expm1_neg(x):
    series = x * (1.0 - x * (0.5 - x * (1.0 / 6 - x * (1.0 / 24 - x * (1.0 / 120 - x * (1.0 / 720))))))
    return jnp.where(x < 0.125, series, 1.0 - jnp.exp(-x))


def scaled_of(rate, residue):
    return residue * jnp.sqrt(minus_expm1_neg(2.0 * rate) * (1.0 / MODES))


def kernel(
    q_hbm, k_hbm, v_hbm, starts, taps_hbm, rate_hbm, residue_hbm, skip, out,
    q_buf, k_buf, v_buf, window, tapbuf, ratebuf, resbuf, line, hline, toep, modal, ends, carry,
    gated, partial, e_buf, recv, prefix, states, decay, no_start,
    in_sem, halo_send, halo_recv, tap_send, tap_recv, mod_send, mod_recv, p1_send, p1_recv, p2_send, p2_recv,
):
    fs = lax.axis_index("fsdp")
    cx = lax.axis_index("ctx")
    dp = lax.axis_index("dp")

    loads = [
        pltpu.make_async_copy(k_hbm.at[0], k_buf, in_sem.at[0]),
        pltpu.make_async_copy(v_hbm.at[0], v_buf, in_sem.at[1]),
        pltpu.make_async_copy(q_hbm.at[0], q_buf, in_sem.at[2]),
    ]
    for load in loads:
        load.start()

    is_mediator = lax.rem(cx, ROW) == 0
    med_block = cx // ROW

    barrier = pltpu.get_barrier_semaphore()

    @pl.when(cx > 0)
    def _():
        pl.semaphore_signal(barrier, inc=1, device_id=(fs, cx - 1, dp), device_id_type=MESH)

    pl.semaphore_signal(barrier, inc=1, device_id=(1 - fs, cx, dp), device_id_type=MESH)
    for d in (1, 2, 3):
        pl.semaphore_signal(
            barrier, inc=1, device_id=(fs, cx, lax.rem(dp + d, 4)), device_id_type=MESH
        )

    @pl.when(is_mediator)
    def _():
        def greet(d, c):
            pl.semaphore_signal(
                barrier, inc=1, device_id=(fs, lax.rem(cx + d, CTX), dp), device_id_type=MESH
            )
            return c

        lax.fori_loop(1, CTX, greet, 0)

    own_row = starts[pl.ds(cx, 1), :].astype(f32)
    before_row = starts[pl.ds(lax.rem(cx + CTX - 1, CTX), 1), :].astype(f32)
    both = jnp.concatenate([before_row, own_row], axis=1)
    t_of = iota((TOK, 2 * TOK), 0)
    s_of = iota((TOK, 2 * TOK), 1)
    at_row = jnp.sum(jnp.where(s_of <= t_of + TOK, both, 0.0), axis=1, keepdims=True)
    upper = one_hot(iota((2 * TOK, 2 * TOK), 0) <= iota((2 * TOK, 2 * TOK), 1))
    counts = dot(jnp.broadcast_to(both, (8, 2 * TOK)).astype(bf16), upper)[0:1]
    first = jnp.where(cx == 0, TOK, 0)
    mask = jnp.where((at_row == counts) & (s_of <= t_of + TOK) & (s_of >= first), 1.0, 0.0)
    before = jnp.sum(before_row, axis=1, keepdims=True)
    total = before + jnp.sum(own_row, axis=1, keepdims=True)
    keep = jnp.where(counts[:, TOK:] == total, 1.0, 0.0)
    continues = jnp.where(at_row == before, 1.0, 0.0)

    loads[0].wait()
    loads[1].wait()
    for j in range(NB):
        cols = pl.ds(j * LANES, LANES)
        window[j, TOK:2 * TOK, :] = (k_buf[:, cols].astype(f32) * v_buf[:, cols].astype(f32)).astype(bf16)
        window[j, 2 * TOK:, :] = jnp.zeros((TOK, LANES), bf16)
        gated[j, :TOK - STRIP, :] = jnp.zeros((TOK - STRIP, LANES), bf16)

    @pl.when(cx == 0)
    def _():
        for j in range(NB):
            window[j, :TOK, :] = jnp.zeros((TOK, LANES), bf16)

    pl.semaphore_wait(barrier, NB + 4 - jnp.where(is_mediator, 1, 0) + jnp.where(cx < CTX - 1, 1, 0))

    halos = [
        pltpu.make_async_remote_copy(
            window.at[j, pl.ds(TOK, TOK)], window.at[j, pl.ds(0, TOK)], halo_send.at[j], halo_recv.at[j],
            device_id=(fs, lax.min(cx + 1, CTX - 1), dp), device_id_type=MESH,
        )
        for j in range(NB)
    ]

    @pl.when(cx < CTX - 1)
    def _():
        for halo in halos:
            halo.start()

    half = lax.rem(dp, 2) * GROUPS
    other = pl.multiple_of(((1 - fs) * 2 + dp // 2) * PAIR, PAIR)
    mine = pl.multiple_of((fs * 2 + dp // 2) * PAIR, PAIR)
    tap_copy = pltpu.make_async_remote_copy(
        taps_hbm.at[:, pl.ds(other, PAIR)], tapbuf.at[fs], tap_send, tap_recv,
        device_id=(1 - fs, cx, dp), device_id_type=MESH,
    )
    tap_copy.start()
    tap_own = pltpu.make_async_copy(taps_hbm.at[:, pl.ds(mine, PAIR)], tapbuf.at[fs], in_sem.at[3])
    tap_own.start()
    modal_copies = []
    for d in (1, 2, 3):
        to = lax.rem(dp + d, 4)
        pair = pl.ds(pl.multiple_of(to // 2 * PAIR, PAIR), PAIR)
        for i, (src, dst) in enumerate(((rate_hbm, ratebuf), (residue_hbm, resbuf))):
            copy = pltpu.make_async_remote_copy(
                src.at[:, pair], dst.at[dp], mod_send.at[i, d - 1], mod_recv.at[i, d - 1],
                device_id=(fs, cx, to), device_id_type=MESH,
            )
            copy.start()
            modal_copies.append(copy)
    pair = pl.ds(pl.multiple_of(dp // 2 * PAIR, PAIR), PAIR)
    rate_own = pltpu.make_async_copy(rate_hbm.at[:, pair], ratebuf.at[dp], in_sem.at[4])
    residue_own = pltpu.make_async_copy(residue_hbm.at[:, pair], resbuf.at[dp], in_sem.at[5])
    rate_own.start()
    residue_own.start()

    tap_own.wait()
    tap_copy.wait()
    flip = [one_hot(iota((TOK // 2, 2 * TOK), 1) == TOK - h * (TOK // 2) - iota((TOK // 2, 2 * TOK), 0)) for h in (0, 1)]
    line[...] = dot_rows(tapbuf[0], flip[0]) + dot_rows(tapbuf[1], flip[1])

    wide_lane = iota((STRIP, 2 * TOK), 1)
    wide_masks = []
    for a in range(STRIPS):
        part = mask[a * STRIP:(a + 1) * STRIP]
        if a:
            part = pltpu.roll(part, 2 * TOK - a * STRIP, 1)
        wide_masks.append(jnp.where(wide_lane < TOK + STRIP, part, 0.0).astype(bf16))

    def build_medium(g, c):
        row = jnp.broadcast_to(line[pl.ds(half + g, 1), :], (STRIP, 2 * TOK))
        base = pltpu.roll(row, 0, 1, stride=1, stride_axis=0).astype(bf16)
        at = pl.ds(pl.multiple_of((g & 15) * STRIP, STRIP), STRIP)
        for a in range(STRIPS):
            toep[(g >> 4) * STRIPS + a, at, :] = base * wide_masks[a]
        return c

    lax.fori_loop(0, GROUPS, build_medium, 0, unroll=8)

    rate_own.wait()
    residue_own.wait()
    for copy in modal_copies:
        copy.wait()

    def gather_modes(buf):
        parts = [dot_rows(buf[d], one_hot(iota((4, MODES), 1) == 4 * d + iota((4, MODES), 0))) for d in range(4)]
        return (parts[0] + parts[1]) + (parts[2] + parts[3])

    rate16 = gather_modes(ratebuf)
    res16 = gather_modes(resbuf)
    repeat = one_hot(half + (iota((GROUPS * MODES, PAIR), 0) >> 4) == iota((GROUPS * MODES, PAIR), 1))
    own_mode = (iota((GROUPS * MODES, MODES), 0) & 15) == iota((GROUPS * MODES, MODES), 1)
    ones = jnp.ones((MODES, TOK), bf16)

    def column(per_group):
        spread = jnp.where(own_mode, dot(repeat, per_group.astype(bf16)), 0.0)
        return dot(spread.astype(bf16), ones)

    rate_col = column(rate16)
    scaled_col = scaled_of(rate_col, column(res16))
    lag = ((TOK - STRIP - iota((1, TOK), 1)) & (TOK - 1)).astype(f32)
    powers = jnp.exp(-rate_col * lag)
    hline[...] = jnp.sum((powers * scaled_col).reshape(GROUPS, MODES, TOK), axis=1)
    ends[...] = (pltpu.roll(powers, STRIP - 1, 1) * keep).astype(bf16)

    lane = iota((STRIP, TOK), 1)
    masks = []
    for a in range(STRIPS):
        part = mask[a * STRIP:(a + 1) * STRIP, TOK:]
        shift = TOK - STRIP - a * STRIP
        if shift:
            part = jnp.where(lane >= shift, pltpu.roll(part, shift, 1), 0.0)
        masks.append(part.astype(bf16))

    def build_modal(g, c):
        row = jnp.broadcast_to(hline[pl.ds(g, 1), :], (STRIP, TOK))
        base = pltpu.roll(row, 0, 1, stride=1, stride_axis=0).astype(bf16)
        at = pl.ds(pl.multiple_of((g & 15) * STRIP, STRIP), STRIP)
        for a in range(STRIPS):
            modal[(g >> 4) * STRIPS + a, at, :] = base * masks[a]
        return c

    lax.fori_loop(0, GROUPS, build_modal, 0, unroll=8)

    tile = one_hot((iota((MODES, GROUPS * MODES), 1) & 15) == iota((MODES, GROUPS * MODES), 0))
    own_group = half + (iota((PAIR, GROUPS * MODES), 1) >> 4) == iota((PAIR, GROUPS * MODES), 0)

    def as_row(per_group):
        spread = jnp.where(own_group, dot(per_group.astype(bf16), tile), 0.0)
        return jnp.sum(spread, axis=0, keepdims=True)

    rate_row = as_row(rate16)
    scaled_row = scaled_of(rate_row, as_row(res16))
    steps = (iota((TOK, 1), 0) + 1).astype(f32)
    carry[...] = (jnp.exp(-rate_row * steps) * scaled_row * continues).astype(bf16)

    @pl.when(is_mediator)
    def _():
        group_of = half + med_block * GB + (iota((PAIR, LANES), 1) >> 4)
        rates = dot_rows(rate16.astype(bf16), one_hot(group_of == iota((PAIR, LANES), 0)))
        decay[...] = jnp.exp(-rates * TOK)
        no_start[...] = jnp.broadcast_to(
            jnp.where(jnp.sum(starts[...], axis=1, keepdims=True) == 0, 1.0, 0.0), (CTX, LANES)
        )

    @pl.when(cx == 0)
    def _():
        states[...] = jnp.zeros((NB, MODES, LANES), bf16)

    same_group = one_hot((iota((LANES, LANES), 0) >> 4) == (iota((LANES, LANES), 1) >> 4))
    loads[2].wait()
    lane_group = iota((1, LANES), 1) >> 4

    def pick(rows, size):
        out_rows = rows[:size]
        for i in range(1, GB):
            out_rows = jnp.where(lane_group == i, rows[i * size:(i + 1) * size], out_rows)
        return out_rows

    for j in range(NB):
        @pl.when(cx > 0)
        def _():
            halos[j].wait_recv()

        medium = jnp.concatenate(
            [pick(dot(toep[j * STRIPS + a], window[j, a * STRIP:a * STRIP + 2 * TOK, :]), STRIP) for a in range(STRIPS)], axis=0
        )
        value = (q_buf[:, j * LANES:(j + 1) * LANES].astype(f32) * medium.astype(bf16).astype(f32)).astype(bf16)
        gated[j, TOK - STRIP:, :] = value
        full = dot(ends[pl.ds(j * GB * MODES, GB * MODES), :], value)
        e_buf[j] = pick(full, MODES).astype(bf16)

        @pl.when(cx != j * ROW)
        def _():
            pltpu.make_async_remote_copy(
                e_buf.at[j], recv.at[cx], p1_send.at[j], p1_recv.at[med_block],
                device_id=(fs, j * ROW, dp), device_id_type=MESH,
            ).start()

        @pl.when(cx == j * ROW)
        def _():
            pltpu.make_async_copy(e_buf.at[j], recv.at[cx], p1_recv.at[j]).start()

    for j in range(NB):
        value = gated[j, TOK - STRIP:, :]
        inside = jnp.concatenate(
            [pick(dot(modal[j * STRIPS + a], gated[j, a * STRIP:a * STRIP + TOK, :]), STRIP) for a in range(STRIPS)], axis=0
        )
        partial[j] = inside + skip[:, j * LANES:(j + 1) * LANES] * value.astype(f32)

    @pl.when(is_mediator)
    def _():
        def return_one(to, c):
            @pl.when(to != cx)
            def _():
                pltpu.make_async_remote_copy(
                    prefix.at[to], states.at[med_block], p2_send, p2_recv.at[med_block],
                    device_id=(fs, to, dp), device_id_type=MESH,
                ).start()

            @pl.when(to == cx)
            def _():
                pltpu.make_async_copy(prefix.at[to], states.at[med_block], p2_recv.at[med_block]).start()

            return c

        total_state = jnp.zeros((MODES, LANES), f32)
        for y in range(CTX // ROW):
            row = pl.ds(y * ROW, ROW)
            pltpu.make_async_copy(recv.at[row], recv.at[row], p1_recv.at[y]).wait()
            for p in range(y * ROW, min((y + 1) * ROW, CTX - 1)):
                total_state = total_state * (decay[...] * no_start[pl.ds(p, 1), :]) + recv[p].astype(f32)
                prefix[p + 1] = total_state.astype(bf16)
            if y + 1 < CTX // ROW:
                return_one((y + 1) * ROW, 0)
            lax.fori_loop(y * ROW + 1, (y + 1) * ROW, return_one, 0)

    for j in range(NB):
        @pl.when(cx > 0)
        def _():
            pltpu.make_async_copy(states.at[j], states.at[j], p2_recv.at[j]).wait()

        spread = jnp.concatenate([states[j]] * GB, axis=0) * same_group
        carried = dot(carry[:, j * LANES:(j + 1) * LANES], spread)
        out[0, :, j * LANES:(j + 1) * LANES] = (partial[j] + carried).astype(bf16)

    @pl.when(cx < CTX - 1)
    def _():
        for halo in halos:
            halo.wait_send()

    for j in range(NB):
        @pl.when(cx != j * ROW)
        def _():
            pltpu.make_async_copy(e_buf.at[j], e_buf.at[j], p1_send.at[j]).wait()

    @pl.when(is_mediator)
    def _():
        def drain(i, c):
            pltpu.make_async_copy(prefix.at[0], prefix.at[0], p2_send).wait()
            return c

        lax.fori_loop(0, jnp.where(cx == 0, CTX - 1, CTX - 2), drain, 0)


def body(query, key, value, starts, taps, rate, residue, skip):
    any_space = pl.BlockSpec(memory_space=pl.ANY)
    vmem = pl.BlockSpec(memory_space=pltpu.VMEM)
    dma = pltpu.SemaphoreType.DMA
    return pl.pallas_call(
        kernel,
        out_shape=jax.ShapeDtypeStruct((1, TOK, WIDE), bf16),
        in_specs=[any_space] * 3 + [vmem] + [any_space] * 3 + [vmem],
        out_specs=vmem,
        scratch_shapes=[
            pltpu.VMEM((TOK, WIDE), bf16),
            pltpu.VMEM((TOK, WIDE), bf16),
            pltpu.VMEM((TOK, WIDE), bf16),
            pltpu.VMEM((NB, 3 * TOK, LANES), bf16),
            pltpu.VMEM((2, TOK // 2, PAIR), bf16),
            pltpu.VMEM((4, 4, PAIR), bf16),
            pltpu.VMEM((4, 4, PAIR), bf16),
            pltpu.VMEM((PAIR, 2 * TOK), f32),
            pltpu.VMEM((GROUPS, TOK), f32),
            pltpu.VMEM((NB * STRIPS, GB * STRIP, 2 * TOK), bf16),
            pltpu.VMEM((NB * STRIPS, GB * STRIP, TOK), bf16),
            pltpu.VMEM((GROUPS * MODES, TOK), bf16),
            pltpu.VMEM((TOK, GROUPS * MODES), bf16),
            pltpu.VMEM((NB, 2 * TOK - STRIP, LANES), bf16),
            pltpu.VMEM((NB, TOK, LANES), f32),
            pltpu.VMEM((NB, MODES, LANES), bf16),
            pltpu.VMEM((CTX, MODES, LANES), bf16),
            pltpu.VMEM((CTX, MODES, LANES), bf16),
            pltpu.VMEM((NB, MODES, LANES), bf16),
            pltpu.VMEM((MODES, LANES), f32),
            pltpu.VMEM((CTX, LANES), f32),
            dma((6,)), dma((NB,)), dma((NB,)), dma, dma, dma((2, 3)), dma((2, 3)),
            dma((NB,)), dma((NB,)), dma, dma((NB,)),
        ],
        compiler_params=pltpu.CompilerParams(
            collective_id=1, has_side_effects=True, vmem_limit_bytes=67_043_328
        ),
    )(query, key, value, starts.reshape(CTX, TOK), taps.T, rate.T, residue.T, skip.reshape(1, WIDE))


def solution(mesh):
    return jax.shard_map(
        body,
        mesh=mesh,
        in_specs=(
            P(None, "ctx", ("fsdp", "dp")),
            P(None, "ctx", ("fsdp", "dp")),
            P(None, "ctx", ("fsdp", "dp")),
            P(),
            P(None, "fsdp"),
            P("fsdp", "dp"),
            P("fsdp", "dp"),
            P(("fsdp", "dp")),
        ),
        out_specs=P(None, "ctx", ("fsdp", "dp")),
        check_vma=False,
    )
```

```python
import functools

import jax
import jax.numpy as jnp
from jax import lax
from jax.experimental import pallas as pl
from jax.experimental.pallas import tpu as pltpu
from jax.sharding import PartitionSpec as P

MESH = pl.DeviceIdType.MESH
CH = 16
MODES = 16
TOK = 128
LANES = 256
GB = LANES // CH
NB = 4
WIDE = NB * LANES
GROUPS = WIDE // CH
PAIR = 2 * GROUPS
CTX = 64
ROW = 16
STRIP = 16
STRIPS = TOK // STRIP

f32 = jnp.float32
bf16 = jnp.bfloat16


def iota(shape, dim):
    return lax.broadcasted_iota(jnp.int32, shape, dim)


def one_hot(cond):
    return jnp.where(cond, 1.0, 0.0).astype(bf16)


def dot(a, b):
    return jnp.dot(a, b, preferred_element_type=f32)


def dot_rows(a, b):
    return lax.dot_general(a, b, (((0,), (0,)), ((), ())), preferred_element_type=f32)


def minus_expm1_neg(x):
    series = x * (1.0 - x * (0.5 - x * (1.0 / 6 - x * (1.0 / 24 - x * (1.0 / 120 - x * (1.0 / 720))))))
    return jnp.where(x < 0.125, series, 1.0 - jnp.exp(-x))


def scaled_of(rate, residue):
    return residue * jnp.sqrt(minus_expm1_neg(2.0 * rate) * (1.0 / MODES))


def kernel(
    q_hbm, k_hbm, v_hbm, starts, taps_hbm, rate_hbm, residue_hbm, skip, out,
    q_buf, k_buf, v_buf, window, tapbuf, ratebuf, resbuf, line, hline, toep, modal, ends, carry,
    gated, partial, e_buf, recv, prefix, states, decay, no_start, powers_buf,
    in_sem, halo_send, halo_recv, tap_send, tap_recv, mod_send, mod_recv, p1_send, p1_recv, p2_send, p2_recv,
):
    fs = lax.axis_index("fsdp")
    cx = lax.axis_index("ctx")
    dp = lax.axis_index("dp")

    loads = [
        pltpu.make_async_copy(k_hbm.at[0], k_buf, in_sem.at[0]),
        pltpu.make_async_copy(v_hbm.at[0], v_buf, in_sem.at[1]),
        pltpu.make_async_copy(q_hbm.at[0], q_buf, in_sem.at[2]),
    ]
    for load in loads:
        load.start()

    is_mediator = lax.rem(cx, ROW) == 0
    med_block = cx // ROW

    barrier = pltpu.get_barrier_semaphore()

    @pl.when(cx > 0)
    def _():
        pl.semaphore_signal(barrier, inc=1, device_id=(fs, cx - 1, dp), device_id_type=MESH)

    pl.semaphore_signal(barrier, inc=1, device_id=(1 - fs, cx, dp), device_id_type=MESH)
    for d in (1, 2, 3):
        pl.semaphore_signal(
            barrier, inc=1, device_id=(fs, cx, lax.rem(dp + d, 4)), device_id_type=MESH
        )

    @pl.when(is_mediator)
    def _():
        def greet(d, c):
            pl.semaphore_signal(
                barrier, inc=1, device_id=(fs, lax.rem(cx + d, CTX), dp), device_id_type=MESH
            )
            return c

        lax.fori_loop(1, CTX, greet, 0)

    own_row = starts[pl.ds(cx, 1), :].astype(f32)
    before_row = starts[pl.ds(lax.rem(cx + CTX - 1, CTX), 1), :].astype(f32)
    both = jnp.concatenate([before_row, own_row], axis=1)
    t_of = iota((TOK, 2 * TOK), 0)
    s_of = iota((TOK, 2 * TOK), 1)
    at_row = jnp.sum(jnp.where(s_of <= t_of + TOK, both, 0.0), axis=1, keepdims=True)
    upper = one_hot(iota((2 * TOK, 2 * TOK), 0) <= iota((2 * TOK, 2 * TOK), 1))
    counts = dot(jnp.broadcast_to(both, (8, 2 * TOK)).astype(bf16), upper)[0:1]
    first = jnp.where(cx == 0, TOK, 0)
    mask = jnp.where((at_row == counts) & (s_of <= t_of + TOK) & (s_of >= first), 1.0, 0.0)
    before = jnp.sum(before_row, axis=1, keepdims=True)
    total = before + jnp.sum(own_row, axis=1, keepdims=True)
    keep = jnp.where(counts[:, TOK:] == total, 1.0, 0.0)
    continues = jnp.where(at_row == before, 1.0, 0.0)

    loads[0].wait()
    loads[1].wait()
    for j in range(NB):
        cols = pl.ds(j * LANES, LANES)
        window[j, TOK:2 * TOK, :] = (k_buf[:, cols].astype(f32) * v_buf[:, cols].astype(f32)).astype(bf16)
        window[j, 2 * TOK:, :] = jnp.zeros((TOK, LANES), bf16)
        gated[j, :TOK - STRIP, :] = jnp.zeros((TOK - STRIP, LANES), bf16)

    @pl.when(cx == 0)
    def _():
        for j in range(NB):
            window[j, :TOK, :] = jnp.zeros((TOK, LANES), bf16)

    pl.semaphore_wait(barrier, NB + 4 - jnp.where(is_mediator, 1, 0) + jnp.where(cx < CTX - 1, 1, 0))

    halos = [
        pltpu.make_async_remote_copy(
            window.at[j, pl.ds(TOK, TOK)], window.at[j, pl.ds(0, TOK)], halo_send.at[j], halo_recv.at[j],
            device_id=(fs, lax.min(cx + 1, CTX - 1), dp), device_id_type=MESH,
        )
        for j in range(NB)
    ]

    @pl.when(cx < CTX - 1)
    def _():
        for halo in halos:
            halo.start()

    half = lax.rem(dp, 2) * GROUPS
    other = pl.multiple_of(((1 - fs) * 2 + dp // 2) * PAIR, PAIR)
    mine = pl.multiple_of((fs * 2 + dp // 2) * PAIR, PAIR)
    tap_copy = pltpu.make_async_remote_copy(
        taps_hbm.at[:, pl.ds(other, PAIR)], tapbuf.at[fs], tap_send, tap_recv,
        device_id=(1 - fs, cx, dp), device_id_type=MESH,
    )
    tap_copy.start()
    tap_own = pltpu.make_async_copy(taps_hbm.at[:, pl.ds(mine, PAIR)], tapbuf.at[fs], in_sem.at[3])
    tap_own.start()
    modal_copies = []
    for d in (1, 2, 3):
        to = lax.rem(dp + d, 4)
        pair = pl.ds(pl.multiple_of(to // 2 * PAIR, PAIR), PAIR)
        for i, (src, dst) in enumerate(((rate_hbm, ratebuf), (residue_hbm, resbuf))):
            copy = pltpu.make_async_remote_copy(
                src.at[:, pair], dst.at[dp], mod_send.at[i, d - 1], mod_recv.at[i, d - 1],
                device_id=(fs, cx, to), device_id_type=MESH,
            )
            copy.start()
            modal_copies.append(copy)
    pair = pl.ds(pl.multiple_of(dp // 2 * PAIR, PAIR), PAIR)
    rate_own = pltpu.make_async_copy(rate_hbm.at[:, pair], ratebuf.at[dp], in_sem.at[4])
    residue_own = pltpu.make_async_copy(residue_hbm.at[:, pair], resbuf.at[dp], in_sem.at[5])
    rate_own.start()
    residue_own.start()

    tap_own.wait()
    tap_copy.wait()
    flip = [one_hot(iota((TOK // 2, 2 * TOK), 1) == TOK - h * (TOK // 2) - iota((TOK // 2, 2 * TOK), 0)) for h in (0, 1)]
    line[...] = dot_rows(tapbuf[0], flip[0]) + dot_rows(tapbuf[1], flip[1])

    wide_lane = iota((STRIP, 2 * TOK), 1)
    wide_masks = []
    for a in range(STRIPS):
        part = mask[a * STRIP:(a + 1) * STRIP]
        if a:
            part = pltpu.roll(part, 2 * TOK - a * STRIP, 1)
        wide_masks.append(jnp.where(wide_lane < TOK + STRIP, part, 0.0).astype(bf16))

    def build_medium(g, c):
        row = jnp.broadcast_to(line[pl.ds(half + g, 1), :], (STRIP, 2 * TOK))
        base = pltpu.roll(row, 0, 1, stride=1, stride_axis=0).astype(bf16)
        at = pl.ds(pl.multiple_of((g & 15) * STRIP, STRIP), STRIP)
        for a in range(STRIPS):
            toep[(g >> 4) * STRIPS + a, at, :] = base * wide_masks[a]
        return c

    lax.fori_loop(0, GROUPS, build_medium, 0, unroll=8)

    rate_own.wait()
    residue_own.wait()
    for copy in modal_copies:
        copy.wait()

    def gather_modes(buf):
        parts = [dot_rows(buf[d], one_hot(iota((4, MODES), 1) == 4 * d + iota((4, MODES), 0))) for d in range(4)]
        return (parts[0] + parts[1]) + (parts[2] + parts[3])

    rate16 = gather_modes(ratebuf)
    res16 = gather_modes(resbuf)
    repeat = one_hot(half + (iota((GROUPS * MODES, PAIR), 0) >> 4) == iota((GROUPS * MODES, PAIR), 1))
    own_mode = (iota((GROUPS * MODES, MODES), 0) & 15) == iota((GROUPS * MODES, MODES), 1)
    ones = jnp.ones((MODES, TOK), bf16)

    def column(per_group):
        spread = jnp.where(own_mode, dot(repeat, per_group.astype(bf16)), 0.0)
        return dot(spread.astype(bf16), ones)

    rate_col = column(rate16)
    lag = ((TOK - STRIP - iota((1, TOK), 1)) & (TOK - 1)).astype(f32)
    powers = jnp.exp(-rate_col * lag)
    powers_buf[...] = powers
    ends[...] = (pltpu.roll(powers, STRIP - 1, 1) * keep).astype(bf16)

    loads[2].wait()
    lane_group = iota((1, LANES), 1) >> 4

    def pick(rows, size):
        out_rows = rows[:size]
        for i in range(1, GB):
            out_rows = jnp.where(lane_group == i, rows[i * size:(i + 1) * size], out_rows)
        return out_rows

    for j in range(NB):
        @pl.when(cx > 0)
        def _():
            halos[j].wait_recv()

        medium = jnp.concatenate(
            [pick(dot(toep[j * STRIPS + a], window[j, a * STRIP:a * STRIP + 2 * TOK, :]), STRIP) for a in range(STRIPS)], axis=0
        )
        value = (q_buf[:, j * LANES:(j + 1) * LANES].astype(f32) * medium.astype(bf16).astype(f32)).astype(bf16)
        gated[j, TOK - STRIP:, :] = value
        full = dot(ends[pl.ds(j * GB * MODES, GB * MODES), :], value)
        e_buf[j] = pick(full, MODES).astype(bf16)

        @pl.when(cx != j * ROW)
        def _():
            pltpu.make_async_remote_copy(
                e_buf.at[j], recv.at[cx], p1_send.at[j], p1_recv.at[med_block],
                device_id=(fs, j * ROW, dp), device_id_type=MESH,
            ).start()

        @pl.when(cx == j * ROW)
        def _():
            pltpu.make_async_copy(e_buf.at[j], recv.at[cx], p1_recv.at[j]).start()

    hline[...] = jnp.sum((powers_buf[...] * scaled_of(rate_col, column(res16))).reshape(GROUPS, MODES, TOK), axis=1)
    lane = iota((STRIP, TOK), 1)
    masks = []
    for a in range(STRIPS):
        part = mask[a * STRIP:(a + 1) * STRIP, TOK:]
        shift = TOK - STRIP - a * STRIP
        if shift:
            part = jnp.where(lane >= shift, pltpu.roll(part, shift, 1), 0.0)
        masks.append(part.astype(bf16))

    def build_modal(g, c):
        row = jnp.broadcast_to(hline[pl.ds(g, 1), :], (STRIP, TOK))
        base = pltpu.roll(row, 0, 1, stride=1, stride_axis=0).astype(bf16)
        at = pl.ds(pl.multiple_of((g & 15) * STRIP, STRIP), STRIP)
        for a in range(STRIPS):
            modal[(g >> 4) * STRIPS + a, at, :] = base * masks[a]
        return c

    lax.fori_loop(0, GROUPS, build_modal, 0, unroll=8)

    tile = one_hot((iota((MODES, GROUPS * MODES), 1) & 15) == iota((MODES, GROUPS * MODES), 0))
    own_group = half + (iota((PAIR, GROUPS * MODES), 1) >> 4) == iota((PAIR, GROUPS * MODES), 0)

    def as_row(per_group):
        spread = jnp.where(own_group, dot(per_group.astype(bf16), tile), 0.0)
        return jnp.sum(spread, axis=0, keepdims=True)

    rate_row = as_row(rate16)
    scaled_row = scaled_of(rate_row, as_row(res16))
    steps = (iota((TOK, 1), 0) + 1).astype(f32)
    carry[...] = (jnp.exp(-rate_row * steps) * scaled_row * continues).astype(bf16)

    @pl.when(is_mediator)
    def _():
        group_of = half + med_block * GB + (iota((PAIR, LANES), 1) >> 4)
        rates = dot_rows(rate16.astype(bf16), one_hot(group_of == iota((PAIR, LANES), 0)))
        decay[...] = jnp.exp(-rates * TOK)
        no_start[...] = jnp.broadcast_to(
            jnp.where(jnp.sum(starts[...], axis=1, keepdims=True) == 0, 1.0, 0.0), (CTX, LANES)
        )

    @pl.when(cx == 0)
    def _():
        states[...] = jnp.zeros((NB, MODES, LANES), bf16)

    same_group = one_hot((iota((LANES, LANES), 0) >> 4) == (iota((LANES, LANES), 1) >> 4))
    for j in range(NB):
        value = gated[j, TOK - STRIP:, :]
        inside = jnp.concatenate(
            [pick(dot(modal[j * STRIPS + a], gated[j, a * STRIP:a * STRIP + TOK, :]), STRIP) for a in range(STRIPS)], axis=0
        )
        partial[j] = inside + skip[:, j * LANES:(j + 1) * LANES] * value.astype(f32)

    @pl.when(is_mediator)
    def _():
        def return_one(to, c):
            @pl.when(to != cx)
            def _():
                pltpu.make_async_remote_copy(
                    prefix.at[to], states.at[med_block], p2_send, p2_recv.at[med_block],
                    device_id=(fs, to, dp), device_id_type=MESH,
                ).start()

            @pl.when(to == cx)
            def _():
                pltpu.make_async_copy(prefix.at[to], states.at[med_block], p2_recv.at[med_block]).start()

            return c

        total_state = jnp.zeros((MODES, LANES), f32)
        for y in range(CTX // ROW):
            row = pl.ds(y * ROW, ROW)
            pltpu.make_async_copy(recv.at[row], recv.at[row], p1_recv.at[y]).wait()
            for p in range(y * ROW, min((y + 1) * ROW, CTX - 1)):
                total_state = total_state * (decay[...] * no_start[pl.ds(p, 1), :]) + recv[p].astype(f32)
                prefix[p + 1] = total_state.astype(bf16)
            if y + 1 < CTX // ROW:
                return_one((y + 1) * ROW, 0)
            lax.fori_loop(y * ROW + 1, (y + 1) * ROW, return_one, 0)

    for j in range(NB):
        @pl.when(cx > 0)
        def _():
            pltpu.make_async_copy(states.at[j], states.at[j], p2_recv.at[j]).wait()

        spread = jnp.concatenate([states[j]] * GB, axis=0) * same_group
        carried = dot(carry[:, j * LANES:(j + 1) * LANES], spread)
        out[0, :, j * LANES:(j + 1) * LANES] = (partial[j] + carried).astype(bf16)

    @pl.when(cx < CTX - 1)
    def _():
        for halo in halos:
            halo.wait_send()

    for j in range(NB):
        @pl.when(cx != j * ROW)
        def _():
            pltpu.make_async_copy(e_buf.at[j], e_buf.at[j], p1_send.at[j]).wait()

    @pl.when(is_mediator)
    def _():
        def drain(i, c):
            pltpu.make_async_copy(prefix.at[0], prefix.at[0], p2_send).wait()
            return c

        lax.fori_loop(0, jnp.where(cx == 0, CTX - 1, CTX - 2), drain, 0)


def body(query, key, value, starts, taps, rate, residue, skip):
    any_space = pl.BlockSpec(memory_space=pltpu.MemorySpace.HBM)
    vmem = pl.BlockSpec(memory_space=pltpu.VMEM)
    dma = pltpu.SemaphoreType.DMA
    return pl.pallas_call(
        kernel,
        out_shape=pltpu.VMEM((1, TOK, WIDE), bf16),
        in_specs=[any_space] * 3 + [vmem] + [any_space] * 3 + [vmem],
        out_specs=vmem,
        scratch_shapes=[
            pltpu.VMEM((TOK, WIDE), bf16),
            pltpu.VMEM((TOK, WIDE), bf16),
            pltpu.VMEM((TOK, WIDE), bf16),
            pltpu.VMEM((NB, 3 * TOK, LANES), bf16),
            pltpu.VMEM((2, TOK // 2, PAIR), bf16),
            pltpu.VMEM((4, 4, PAIR), bf16),
            pltpu.VMEM((4, 4, PAIR), bf16),
            pltpu.VMEM((PAIR, 2 * TOK), f32),
            pltpu.VMEM((GROUPS, TOK), f32),
            pltpu.VMEM((NB * STRIPS, GB * STRIP, 2 * TOK), bf16),
            pltpu.VMEM((NB * STRIPS, GB * STRIP, TOK), bf16),
            pltpu.VMEM((GROUPS * MODES, TOK), bf16),
            pltpu.VMEM((TOK, GROUPS * MODES), bf16),
            pltpu.VMEM((NB, 2 * TOK - STRIP, LANES), bf16),
            pltpu.VMEM((NB, TOK, LANES), f32),
            pltpu.VMEM((NB, MODES, LANES), bf16),
            pltpu.VMEM((CTX, MODES, LANES), bf16),
            pltpu.VMEM((CTX, MODES, LANES), bf16),
            pltpu.VMEM((NB, MODES, LANES), bf16),
            pltpu.VMEM((MODES, LANES), f32),
            pltpu.VMEM((CTX, LANES), f32),
            pltpu.VMEM((GROUPS * MODES, TOK), f32),
            dma((6,)), dma((NB,)), dma((NB,)), dma, dma, dma((2, 3)), dma((2, 3)),
            dma((NB,)), dma((NB,)), dma, dma((NB,)),
        ],
        compiler_params=pltpu.CompilerParams(
            collective_id=1, has_side_effects=True, vmem_limit_bytes=60000000
        ),
    )(query, key, value, starts.reshape(CTX, TOK), taps.T, rate.T, residue.T, skip.reshape(1, WIDE))


def solution(mesh):
    return jax.shard_map(
        body,
        mesh=mesh,
        in_specs=(
            P(None, "ctx", ("fsdp", "dp")),
            P(None, "ctx", ("fsdp", "dp")),
            P(None, "ctx", ("fsdp", "dp")),
            P(),
            P(None, "fsdp"),
            P("fsdp", "dp"),
            P("fsdp", "dp"),
            P(("fsdp", "dp")),
        ),
        out_specs=P(None, "ctx", ("fsdp", "dp")),
        check_vma=False,
    )
```

```python
import functools

import jax
import jax.numpy as jnp
from jax import lax
from jax.experimental import pallas as pl
from jax.experimental.pallas import tpu as pltpu
from jax.sharding import PartitionSpec as P

MESH = pl.DeviceIdType.MESH
CH = 16
MODES = 16
TOK = 128
LANES = 256
GB = LANES // CH
NB = 4
WIDE = NB * LANES
GROUPS = WIDE // CH
PAIR = 2 * GROUPS
CTX = 64
ROW = 16
SEAT = 1
STRIP = 16
STRIPS = TOK // STRIP

f32 = jnp.float32
bf16 = jnp.bfloat16


def iota(shape, dim):
    return lax.broadcasted_iota(jnp.int32, shape, dim)


def one_hot(cond):
    return jnp.where(cond, 1.0, 0.0).astype(bf16)


def dot(a, b):
    return jnp.dot(a, b, preferred_element_type=f32)


def dot_rows(a, b):
    return lax.dot_general(a, b, (((0,), (0,)), ((), ())), preferred_element_type=f32)


def minus_expm1_neg(x):
    series = x * (1.0 - x * (0.5 - x * (1.0 / 6 - x * (1.0 / 24 - x * (1.0 / 120 - x * (1.0 / 720))))))
    return jnp.where(x < 0.125, series, 1.0 - jnp.exp(-x))


def scaled_of(rate, residue):
    return residue * jnp.sqrt(minus_expm1_neg(2.0 * rate) * (1.0 / MODES))


def kernel(
    q_hbm, k_hbm, v_hbm, starts, taps_hbm, rate_hbm, residue_hbm, skip, out,
    q_buf, k_buf, v_buf, window, tapbuf, ratebuf, resbuf, line, hline, toep, modal, ends, carry,
    gated, partial, e_buf, recv, prefix, states, decay, no_start, powers_buf,
    in_sem, halo_send, halo_recv, tap_send, tap_recv, mod_send, mod_recv, p1_send, p1_recv, p2_send, p2_recv,
):
    fs = lax.axis_index("fsdp")
    cx = lax.axis_index("ctx")
    dp = lax.axis_index("dp")

    loads = [
        pltpu.make_async_copy(k_hbm.at[0], k_buf, in_sem.at[0]),
        pltpu.make_async_copy(v_hbm.at[0], v_buf, in_sem.at[1]),
        pltpu.make_async_copy(q_hbm.at[0], q_buf, in_sem.at[2]),
    ]
    for load in loads:
        load.start()

    is_mediator = lax.rem(cx, ROW) == SEAT
    opens_row = (lax.rem(cx, ROW) == 0) & (cx > 0)
    med_block = cx // ROW

    barrier = pltpu.get_barrier_semaphore()

    @pl.when(cx > 0)
    def _():
        pl.semaphore_signal(barrier, inc=1, device_id=(fs, cx - 1, dp), device_id_type=MESH)

    pl.semaphore_signal(barrier, inc=1, device_id=(1 - fs, cx, dp), device_id_type=MESH)
    for d in (1, 2, 3):
        pl.semaphore_signal(
            barrier, inc=1, device_id=(fs, cx, lax.rem(dp + d, 4)), device_id_type=MESH
        )

    @pl.when(is_mediator)
    def _():
        def greet(d, c):
            pl.semaphore_signal(
                barrier, inc=1, device_id=(fs, lax.rem(cx + d, CTX), dp), device_id_type=MESH
            )
            return c

        lax.fori_loop(1, CTX, greet, 0)

    @pl.when(opens_row)
    def _():
        for j in range(NB):
            pl.semaphore_signal(
                barrier, inc=1, device_id=(fs, j * ROW + SEAT, dp), device_id_type=MESH
            )

    own_row = starts[pl.ds(cx, 1), :].astype(f32)
    before_row = starts[pl.ds(lax.rem(cx + CTX - 1, CTX), 1), :].astype(f32)
    both = jnp.concatenate([before_row, own_row], axis=1)
    t_of = iota((TOK, 2 * TOK), 0)
    s_of = iota((TOK, 2 * TOK), 1)
    at_row = jnp.sum(jnp.where(s_of <= t_of + TOK, both, 0.0), axis=1, keepdims=True)
    upper = one_hot(iota((2 * TOK, 2 * TOK), 0) <= iota((2 * TOK, 2 * TOK), 1))
    counts = dot(jnp.broadcast_to(both, (8, 2 * TOK)).astype(bf16), upper)[0:1]
    first = jnp.where(cx == 0, TOK, 0)
    mask = jnp.where((at_row == counts) & (s_of <= t_of + TOK) & (s_of >= first), 1.0, 0.0)
    before = jnp.sum(before_row, axis=1, keepdims=True)
    total = before + jnp.sum(own_row, axis=1, keepdims=True)
    keep = jnp.where(counts[:, TOK:] == total, 1.0, 0.0)
    continues = jnp.where(at_row == before, 1.0, 0.0)

    loads[0].wait()
    loads[1].wait()
    for j in range(NB):
        cols = pl.ds(j * LANES, LANES)
        window[j, TOK:2 * TOK, :] = (k_buf[:, cols].astype(f32) * v_buf[:, cols].astype(f32)).astype(bf16)
        window[j, 2 * TOK:, :] = jnp.zeros((TOK, LANES), bf16)
        gated[j, :TOK - STRIP, :] = jnp.zeros((TOK - STRIP, LANES), bf16)

    @pl.when(cx == 0)
    def _():
        for j in range(NB):
            window[j, :TOK, :] = jnp.zeros((TOK, LANES), bf16)

    pl.semaphore_wait(barrier, NB + 4 + jnp.where(is_mediator, CTX // ROW - 2, 0) + jnp.where(cx < CTX - 1, 1, 0))

    halos = [
        pltpu.make_async_remote_copy(
            window.at[j, pl.ds(TOK, TOK)], window.at[j, pl.ds(0, TOK)], halo_send.at[j], halo_recv.at[j],
            device_id=(fs, lax.min(cx + 1, CTX - 1), dp), device_id_type=MESH,
        )
        for j in range(NB)
    ]

    @pl.when(cx < CTX - 1)
    def _():
        for halo in halos:
            halo.start()

    half = lax.rem(dp, 2) * GROUPS
    other = pl.multiple_of(((1 - fs) * 2 + dp // 2) * PAIR, PAIR)
    mine = pl.multiple_of((fs * 2 + dp // 2) * PAIR, PAIR)
    tap_copy = pltpu.make_async_remote_copy(
        taps_hbm.at[:, pl.ds(other, PAIR)], tapbuf.at[fs], tap_send, tap_recv,
        device_id=(1 - fs, cx, dp), device_id_type=MESH,
    )
    tap_copy.start()
    tap_own = pltpu.make_async_copy(taps_hbm.at[:, pl.ds(mine, PAIR)], tapbuf.at[fs], in_sem.at[3])
    tap_own.start()
    modal_copies = []
    for d in (1, 2, 3):
        to = lax.rem(dp + d, 4)
        pair = pl.ds(pl.multiple_of(to // 2 * PAIR, PAIR), PAIR)
        for i, (src, dst) in enumerate(((rate_hbm, ratebuf), (residue_hbm, resbuf))):
            copy = pltpu.make_async_remote_copy(
                src.at[:, pair], dst.at[dp], mod_send.at[i, d - 1], mod_recv.at[i, d - 1],
                device_id=(fs, cx, to), device_id_type=MESH,
            )
            copy.start()
            modal_copies.append(copy)
    pair = pl.ds(pl.multiple_of(dp // 2 * PAIR, PAIR), PAIR)
    rate_own = pltpu.make_async_copy(rate_hbm.at[:, pair], ratebuf.at[dp], in_sem.at[4])
    residue_own = pltpu.make_async_copy(residue_hbm.at[:, pair], resbuf.at[dp], in_sem.at[5])
    rate_own.start()
    residue_own.start()

    tap_own.wait()
    tap_copy.wait()
    flip = [one_hot(iota((TOK // 2, 2 * TOK), 1) == TOK - h * (TOK // 2) - iota((TOK // 2, 2 * TOK), 0)) for h in (0, 1)]
    line[...] = dot_rows(tapbuf[0], flip[0]) + dot_rows(tapbuf[1], flip[1])

    wide_lane = iota((STRIP, 2 * TOK), 1)
    wide_masks = []
    for a in range(STRIPS):
        part = mask[a * STRIP:(a + 1) * STRIP]
        if a:
            part = pltpu.roll(part, 2 * TOK - a * STRIP, 1)
        wide_masks.append(jnp.where(wide_lane < TOK + STRIP, part, 0.0).astype(bf16))

    def build_medium(g, c):
        row = jnp.broadcast_to(line[pl.ds(half + g, 1), :], (STRIP, 2 * TOK))
        base = pltpu.roll(row, 0, 1, stride=1, stride_axis=0).astype(bf16)
        at = pl.ds(pl.multiple_of((g & 15) * STRIP, STRIP), STRIP)
        for a in range(STRIPS):
            toep[(g >> 4) * STRIPS + a, at, :] = base * wide_masks[a]
        return c

    lax.fori_loop(0, GROUPS, build_medium, 0, unroll=16)

    rate_own.wait()
    residue_own.wait()
    for copy in modal_copies:
        copy.wait()

    def gather_modes(buf):
        parts = [dot_rows(buf[d], one_hot(iota((4, MODES), 1) == 4 * d + iota((4, MODES), 0))) for d in range(4)]
        return (parts[0] + parts[1]) + (parts[2] + parts[3])

    rate16 = gather_modes(ratebuf)
    res16 = gather_modes(resbuf)
    repeat = one_hot(half + (iota((GROUPS * MODES, PAIR), 0) >> 4) == iota((GROUPS * MODES, PAIR), 1))
    own_mode = (iota((GROUPS * MODES, MODES), 0) & 15) == iota((GROUPS * MODES, MODES), 1)
    ones = jnp.ones((MODES, TOK), bf16)

    def column(per_group):
        spread = jnp.where(own_mode, dot(repeat, per_group.astype(bf16)), 0.0)
        return dot(spread.astype(bf16), ones)

    rate_col = column(rate16)
    lag = ((TOK - STRIP - iota((1, TOK), 1)) & (TOK - 1)).astype(f32)
    powers = jnp.exp(-rate_col * lag)
    powers_buf[...] = powers
    ends[...] = (pltpu.roll(powers, STRIP - 1, 1) * keep).astype(bf16)

    loads[2].wait()
    lane_group = iota((1, LANES), 1) >> 4

    def pick(rows, size):
        out_rows = rows[:size]
        for i in range(1, GB):
            out_rows = jnp.where(lane_group == i, rows[i * size:(i + 1) * size], out_rows)
        return out_rows

    for j in range(NB):
        @pl.when(cx > 0)
        def _():
            halos[j].wait_recv()

        medium = jnp.concatenate(
            [pick(dot(toep[j * STRIPS + a], window[j, a * STRIP:a * STRIP + 2 * TOK, :]), STRIP) for a in range(STRIPS)], axis=0
        )
        value = (q_buf[:, j * LANES:(j + 1) * LANES].astype(f32) * medium.astype(bf16).astype(f32)).astype(bf16)
        gated[j, TOK - STRIP:, :] = value
        full = dot(ends[pl.ds(j * GB * MODES, GB * MODES), :], value)
        e_buf[j] = pick(full, MODES).astype(bf16)

        @pl.when(cx != j * ROW + SEAT)
        def _():
            pltpu.make_async_remote_copy(
                e_buf.at[j], recv.at[cx], p1_send.at[j], p1_recv.at[med_block],
                device_id=(fs, j * ROW + SEAT, dp), device_id_type=MESH,
            ).start()

        @pl.when(cx == j * ROW + SEAT)
        def _():
            pltpu.make_async_copy(e_buf.at[j], recv.at[cx], p1_recv.at[j]).start()

    hline[...] = jnp.sum((powers_buf[...] * scaled_of(rate_col, column(res16))).reshape(GROUPS, MODES, TOK), axis=1)
    lane = iota((STRIP, TOK), 1)
    masks = []
    for a in range(STRIPS):
        part = mask[a * STRIP:(a + 1) * STRIP, TOK:]
        shift = TOK - STRIP - a * STRIP
        if shift:
            part = jnp.where(lane >= shift, pltpu.roll(part, shift, 1), 0.0)
        masks.append(part.astype(bf16))

    def build_modal(g, c):
        row = jnp.broadcast_to(hline[pl.ds(g, 1), :], (STRIP, TOK))
        base = pltpu.roll(row, 0, 1, stride=1, stride_axis=0).astype(bf16)
        at = pl.ds(pl.multiple_of((g & 15) * STRIP, STRIP), STRIP)
        for a in range(STRIPS):
            modal[(g >> 4) * STRIPS + a, at, :] = base * masks[a]
        return c

    lax.fori_loop(0, GROUPS, build_modal, 0, unroll=16)

    tile = one_hot((iota((MODES, GROUPS * MODES), 1) & 15) == iota((MODES, GROUPS * MODES), 0))
    own_group = half + (iota((PAIR, GROUPS * MODES), 1) >> 4) == iota((PAIR, GROUPS * MODES), 0)

    def as_row(per_group):
        spread = jnp.where(own_group, dot(per_group.astype(bf16), tile), 0.0)
        return jnp.sum(spread, axis=0, keepdims=True)

    rate_row = as_row(rate16)
    scaled_row = scaled_of(rate_row, as_row(res16))
    steps = (iota((TOK, 1), 0) + 1).astype(f32)
    carry[...] = (jnp.exp(-rate_row * steps) * scaled_row * continues).astype(bf16)

    @pl.when(is_mediator)
    def _():
        group_of = half + med_block * GB + (iota((PAIR, LANES), 1) >> 4)
        rates = dot_rows(rate16.astype(bf16), one_hot(group_of == iota((PAIR, LANES), 0)))
        decay[...] = jnp.exp(-rates * TOK)
        no_start[...] = jnp.broadcast_to(
            jnp.where(jnp.sum(starts[...], axis=1, keepdims=True) == 0, 1.0, 0.0), (CTX, LANES)
        )

    @pl.when(cx == 0)
    def _():
        states[...] = jnp.zeros((NB, MODES, LANES), bf16)

    same_group = one_hot((iota((LANES, LANES), 0) >> 4) == (iota((LANES, LANES), 1) >> 4))
    for j in range(NB):
        value = gated[j, TOK - STRIP:, :]
        inside = jnp.concatenate(
            [pick(dot(modal[j * STRIPS + a], gated[j, a * STRIP:a * STRIP + TOK, :]), STRIP) for a in range(STRIPS)], axis=0
        )
        partial[j] = inside + skip[:, j * LANES:(j + 1) * LANES] * value.astype(f32)

    @pl.when(is_mediator)
    def _():
        def return_one(to, c):
            @pl.when(to != cx)
            def _():
                pltpu.make_async_remote_copy(
                    prefix.at[to], states.at[med_block], p2_send, p2_recv.at[med_block],
                    device_id=(fs, to, dp), device_id_type=MESH,
                ).start()

            @pl.when(to == cx)
            def _():
                pltpu.make_async_copy(prefix.at[to], states.at[med_block], p2_recv.at[med_block]).start()

            return c

        total_state = jnp.zeros((MODES, LANES), f32)
        for y in range(CTX // ROW):
            row = pl.ds(y * ROW, ROW)
            pltpu.make_async_copy(recv.at[row], recv.at[row], p1_recv.at[y]).wait()
            for p in range(y * ROW, min((y + 1) * ROW, CTX - 1)):
                total_state = total_state * (decay[...] * no_start[pl.ds(p, 1), :]) + recv[p].astype(f32)
                prefix[p + 1] = total_state.astype(bf16)
            if y + 1 < CTX // ROW:
                return_one((y + 1) * ROW, 0)
            lax.fori_loop(y * ROW + 1, (y + 1) * ROW, return_one, 0)

    for j in range(NB):
        @pl.when(cx > 0)
        def _():
            pltpu.make_async_copy(states.at[j], states.at[j], p2_recv.at[j]).wait()

        spread = jnp.concatenate([states[j]] * GB, axis=0) * same_group
        carried = dot(carry[:, j * LANES:(j + 1) * LANES], spread)
        out[0, :, j * LANES:(j + 1) * LANES] = (partial[j] + carried).astype(bf16)

    @pl.when(cx < CTX - 1)
    def _():
        for halo in halos:
            halo.wait_send()

    for j in range(NB):
        @pl.when(cx != j * ROW + SEAT)
        def _():
            pltpu.make_async_copy(e_buf.at[j], e_buf.at[j], p1_send.at[j]).wait()

    @pl.when(is_mediator)
    def _():
        def drain(i, c):
            pltpu.make_async_copy(prefix.at[0], prefix.at[0], p2_send).wait()
            return c

        lax.fori_loop(0, CTX - 2, drain, 0)


def body(query, key, value, starts, taps, rate, residue, skip):
    any_space = pl.BlockSpec(memory_space=pltpu.MemorySpace.HBM)
    vmem = pl.BlockSpec(memory_space=pltpu.VMEM)
    dma = pltpu.SemaphoreType.DMA
    return pl.pallas_call(
        kernel,
        out_shape=pltpu.VMEM((1, TOK, WIDE), bf16),
        in_specs=[any_space] * 3 + [vmem] + [any_space] * 3 + [vmem],
        out_specs=vmem,
        scratch_shapes=[
            pltpu.VMEM((TOK, WIDE), bf16),
            pltpu.VMEM((TOK, WIDE), bf16),
            pltpu.VMEM((TOK, WIDE), bf16),
            pltpu.VMEM((NB, 3 * TOK, LANES), bf16),
            pltpu.VMEM((2, TOK // 2, PAIR), bf16),
            pltpu.VMEM((4, 4, PAIR), bf16),
            pltpu.VMEM((4, 4, PAIR), bf16),
            pltpu.VMEM((PAIR, 2 * TOK), f32),
            pltpu.VMEM((GROUPS, TOK), f32),
            pltpu.VMEM((NB * STRIPS, GB * STRIP, 2 * TOK), bf16),
            pltpu.VMEM((NB * STRIPS, GB * STRIP, TOK), bf16),
            pltpu.VMEM((GROUPS * MODES, TOK), bf16),
            pltpu.VMEM((TOK, GROUPS * MODES), bf16),
            pltpu.VMEM((NB, 2 * TOK - STRIP, LANES), bf16),
            pltpu.VMEM((NB, TOK, LANES), f32),
            pltpu.VMEM((NB, MODES, LANES), bf16),
            pltpu.VMEM((CTX, MODES, LANES), bf16),
            pltpu.VMEM((CTX, MODES, LANES), bf16),
            pltpu.VMEM((NB, MODES, LANES), bf16),
            pltpu.VMEM((MODES, LANES), f32),
            pltpu.VMEM((CTX, LANES), f32),
            pltpu.VMEM((GROUPS * MODES, TOK), f32),
            dma((6,)), dma((NB,)), dma((NB,)), dma, dma, dma((2, 3)), dma((2, 3)),
            dma((NB,)), dma((NB,)), dma, dma((NB,)),
        ],
        compiler_params=pltpu.CompilerParams(
            collective_id=1, has_side_effects=True, vmem_limit_bytes=60000000
        ),
    )(query, key, value, starts.reshape(CTX, TOK), taps.T, rate.T, residue.T, skip.reshape(1, WIDE))


def solution(mesh):
    return jax.shard_map(
        body,
        mesh=mesh,
        in_specs=(
            P(None, "ctx", ("fsdp", "dp")),
            P(None, "ctx", ("fsdp", "dp")),
            P(None, "ctx", ("fsdp", "dp")),
            P(),
            P(None, "fsdp"),
            P("fsdp", "dp"),
            P("fsdp", "dp"),
            P(("fsdp", "dp")),
        ),
        out_specs=P(None, "ctx", ("fsdp", "dp")),
        check_vma=False,
    )
```

```python
import functools

import jax
import jax.numpy as jnp
from jax import lax
from jax.experimental import pallas as pl
from jax.experimental.pallas import tpu as pltpu
from jax.sharding import PartitionSpec as P

MESH = pl.DeviceIdType.MESH
CH = 16
MODES = 16
TOK = 128
LANES = 256
GB = LANES // CH
NB = 4
WIDE = NB * LANES
GROUPS = WIDE // CH
PAIR = 2 * GROUPS
CTX = 64
ROW = 16
PART = 8
STRIP = 16
STRIPS = TOK // STRIP

f32 = jnp.float32
bf16 = jnp.bfloat16


def iota(shape, dim):
    return lax.broadcasted_iota(jnp.int32, shape, dim)


def one_hot(cond):
    return jnp.where(cond, 1.0, 0.0).astype(bf16)


def dot(a, b):
    return jnp.dot(a, b, preferred_element_type=f32)


def dot_rows(a, b):
    return lax.dot_general(a, b, (((0,), (0,)), ((), ())), preferred_element_type=f32)


def minus_expm1_neg(x):
    series = x * (1.0 - x * (0.5 - x * (1.0 / 6 - x * (1.0 / 24 - x * (1.0 / 120 - x * (1.0 / 720))))))
    return jnp.where(x < 0.125, series, 1.0 - jnp.exp(-x))


def scaled_of(rate, residue):
    return residue * jnp.sqrt(minus_expm1_neg(2.0 * rate) * (1.0 / MODES))


def kernel(
    q_hbm, k_hbm, v_hbm, starts, taps_hbm, rate_hbm, residue_hbm, skip, out,
    q_buf, k_buf, v_buf, window, tapbuf, ratebuf, resbuf, line, hline, toep, modal, ends, carry,
    gated, partial, e_buf, recv, prefix, states, decay, no_start, powers_buf,
    in_sem, halo_send, halo_recv, tap_send, tap_recv, mod_send, mod_recv, p1_send, p1_recv, p2_send, p2_recv,
):
    fs = lax.axis_index("fsdp")
    cx = lax.axis_index("ctx")
    dp = lax.axis_index("dp")

    loads = [
        pltpu.make_async_copy(k_hbm.at[0], k_buf, in_sem.at[0]),
        pltpu.make_async_copy(v_hbm.at[0], v_buf, in_sem.at[1]),
        pltpu.make_async_copy(q_hbm.at[0], q_buf, in_sem.at[2]),
    ]
    for load in loads:
        load.start()

    is_mediator = lax.rem(cx, ROW) == 0
    med_block = cx // ROW
    part_of = cx // PART

    barrier = pltpu.get_barrier_semaphore()

    @pl.when(cx > 0)
    def _():
        pl.semaphore_signal(barrier, inc=1, device_id=(fs, cx - 1, dp), device_id_type=MESH)

    pl.semaphore_signal(barrier, inc=1, device_id=(1 - fs, cx, dp), device_id_type=MESH)
    for d in (1, 2, 3):
        pl.semaphore_signal(
            barrier, inc=1, device_id=(fs, cx, lax.rem(dp + d, 4)), device_id_type=MESH
        )

    @pl.when(is_mediator)
    def _():
        def greet(d, c):
            pl.semaphore_signal(
                barrier, inc=1, device_id=(fs, lax.rem(cx + d, CTX), dp), device_id_type=MESH
            )
            return c

        lax.fori_loop(1, CTX, greet, 0)

    own_row = starts[pl.ds(cx, 1), :].astype(f32)
    before_row = starts[pl.ds(lax.rem(cx + CTX - 1, CTX), 1), :].astype(f32)
    both = jnp.concatenate([before_row, own_row], axis=1)
    t_of = iota((TOK, 2 * TOK), 0)
    s_of = iota((TOK, 2 * TOK), 1)
    at_row = jnp.sum(jnp.where(s_of <= t_of + TOK, both, 0.0), axis=1, keepdims=True)
    upper = one_hot(iota((2 * TOK, 2 * TOK), 0) <= iota((2 * TOK, 2 * TOK), 1))
    counts = dot(jnp.broadcast_to(both, (8, 2 * TOK)).astype(bf16), upper)[0:1]
    first = jnp.where(cx == 0, TOK, 0)
    mask = jnp.where((at_row == counts) & (s_of <= t_of + TOK) & (s_of >= first), 1.0, 0.0)
    before = jnp.sum(before_row, axis=1, keepdims=True)
    total = before + jnp.sum(own_row, axis=1, keepdims=True)
    keep = jnp.where(counts[:, TOK:] == total, 1.0, 0.0)
    continues = jnp.where(at_row == before, 1.0, 0.0)

    loads[0].wait()
    loads[1].wait()
    for j in range(NB):
        cols = pl.ds(j * LANES, LANES)
        window[j, TOK:2 * TOK, :] = (k_buf[:, cols].astype(f32) * v_buf[:, cols].astype(f32)).astype(bf16)
        window[j, 2 * TOK:, :] = jnp.zeros((TOK, LANES), bf16)
        gated[j, :TOK - STRIP, :] = jnp.zeros((TOK - STRIP, LANES), bf16)

    @pl.when(cx == 0)
    def _():
        for j in range(NB):
            window[j, :TOK, :] = jnp.zeros((TOK, LANES), bf16)

    pl.semaphore_wait(barrier, NB + 4 - jnp.where(is_mediator, 1, 0) + jnp.where(cx < CTX - 1, 1, 0))

    def order(row):
        return [lax.rem(row + d, NB) for d in (2, 3, 1, 0)]

    def halo_copies(row):
        return [
            pltpu.make_async_remote_copy(
                window.at[j, pl.ds(TOK, TOK)], window.at[j, pl.ds(0, TOK)], halo_send.at[j], halo_recv.at[j],
                device_id=(fs, lax.rem(cx + 1, CTX), dp), device_id_type=MESH,
            )
            for j in order(row)
        ]

    halos = halo_copies(lax.rem(cx + 1, CTX) // ROW)
    arriving = halo_copies(med_block)

    @pl.when(cx < CTX - 1)
    def _():
        for halo in halos:
            halo.start()

    half = lax.rem(dp, 2) * GROUPS
    other = pl.multiple_of(((1 - fs) * 2 + dp // 2) * PAIR, PAIR)
    mine = pl.multiple_of((fs * 2 + dp // 2) * PAIR, PAIR)
    tap_copy = pltpu.make_async_remote_copy(
        taps_hbm.at[:, pl.ds(other, PAIR)], tapbuf.at[fs], tap_send, tap_recv,
        device_id=(1 - fs, cx, dp), device_id_type=MESH,
    )
    tap_copy.start()
    tap_own = pltpu.make_async_copy(taps_hbm.at[:, pl.ds(mine, PAIR)], tapbuf.at[fs], in_sem.at[3])
    tap_own.start()
    modal_copies = []
    for d in (1, 2, 3):
        to = lax.rem(dp + d, 4)
        pair = pl.ds(pl.multiple_of(to // 2 * PAIR, PAIR), PAIR)
        for i, (src, dst) in enumerate(((rate_hbm, ratebuf), (residue_hbm, resbuf))):
            copy = pltpu.make_async_remote_copy(
                src.at[:, pair], dst.at[dp], mod_send.at[i, d - 1], mod_recv.at[i, d - 1],
                device_id=(fs, cx, to), device_id_type=MESH,
            )
            copy.start()
            modal_copies.append(copy)
    pair = pl.ds(pl.multiple_of(dp // 2 * PAIR, PAIR), PAIR)
    rate_own = pltpu.make_async_copy(rate_hbm.at[:, pair], ratebuf.at[dp], in_sem.at[4])
    residue_own = pltpu.make_async_copy(residue_hbm.at[:, pair], resbuf.at[dp], in_sem.at[5])
    rate_own.start()
    residue_own.start()

    tap_own.wait()
    tap_copy.wait()
    flip = [one_hot(iota((TOK // 2, 2 * TOK), 1) == TOK - h * (TOK // 2) - iota((TOK // 2, 2 * TOK), 0)) for h in (0, 1)]
    line[...] = dot_rows(tapbuf[0], flip[0]) + dot_rows(tapbuf[1], flip[1])

    wide_lane = iota((STRIP, 2 * TOK), 1)
    wide_masks = []
    for a in range(STRIPS):
        part = mask[a * STRIP:(a + 1) * STRIP]
        if a:
            part = pltpu.roll(part, 2 * TOK - a * STRIP, 1)
        wide_masks.append(jnp.where(wide_lane < TOK + STRIP, part, 0.0).astype(bf16))

    def build_medium(g, c):
        row = jnp.broadcast_to(line[pl.ds(half + g, 1), :], (STRIP, 2 * TOK))
        base = pltpu.roll(row, 0, 1, stride=1, stride_axis=0).astype(bf16)
        at = pl.ds(pl.multiple_of((g & 15) * STRIP, STRIP), STRIP)
        for a in range(STRIPS):
            toep[(g >> 4) * STRIPS + a, at, :] = base * wide_masks[a]
        return c

    lax.fori_loop(0, GROUPS, build_medium, 0, unroll=16)

    rate_own.wait()
    residue_own.wait()
    for copy in modal_copies:
        copy.wait()

    def gather_modes(buf):
        parts = [dot_rows(buf[d], one_hot(iota((4, MODES), 1) == 4 * d + iota((4, MODES), 0))) for d in range(4)]
        return (parts[0] + parts[1]) + (parts[2] + parts[3])

    rate16 = gather_modes(ratebuf)
    res16 = gather_modes(resbuf)
    repeat = one_hot(half + (iota((GROUPS * MODES, PAIR), 0) >> 4) == iota((GROUPS * MODES, PAIR), 1))
    own_mode = (iota((GROUPS * MODES, MODES), 0) & 15) == iota((GROUPS * MODES, MODES), 1)
    ones = jnp.ones((MODES, TOK), bf16)

    def column(per_group):
        spread = jnp.where(own_mode, dot(repeat, per_group.astype(bf16)), 0.0)
        return dot(spread.astype(bf16), ones)

    rate_col = column(rate16)
    lag = ((TOK - STRIP - iota((1, TOK), 1)) & (TOK - 1)).astype(f32)
    powers = jnp.exp(-rate_col * lag)
    powers_buf[...] = powers
    ends[...] = (pltpu.roll(powers, STRIP - 1, 1) * keep).astype(bf16)

    loads[2].wait()
    lane_group = iota((1, LANES), 1) >> 4

    def pick(rows, size):
        out_rows = rows[:size]
        for i in range(1, GB):
            out_rows = jnp.where(lane_group == i, rows[i * size:(i + 1) * size], out_rows)
        return out_rows

    for i, j in enumerate(order(med_block)):
        @pl.when(cx > 0)
        def _():
            arriving[i].wait_recv()

        medium = jnp.concatenate(
            [pick(dot(toep[j * STRIPS + a], window[j, a * STRIP:a * STRIP + 2 * TOK, :]), STRIP) for a in range(STRIPS)], axis=0
        )
        value = (q_buf[:, pl.ds(pl.multiple_of(j * LANES, LANES), LANES)].astype(f32) * medium.astype(bf16).astype(f32)).astype(bf16)
        gated[j, TOK - STRIP:, :] = value
        full = dot(ends[pl.ds(pl.multiple_of(j * GB * MODES, GB * MODES), GB * MODES), :], value)
        e_buf[j] = pick(full, MODES).astype(bf16)

        @pl.when(cx != j * ROW)
        def _():
            pltpu.make_async_remote_copy(
                e_buf.at[j], recv.at[cx], p1_send.at[j], p1_recv.at[part_of],
                device_id=(fs, j * ROW, dp), device_id_type=MESH,
            ).start()

        @pl.when(cx == j * ROW)
        def _():
            pltpu.make_async_copy(e_buf.at[j], recv.at[cx], p1_recv.at[part_of]).start()

    hline[...] = jnp.sum((powers_buf[...] * scaled_of(rate_col, column(res16))).reshape(GROUPS, MODES, TOK), axis=1)
    lane = iota((STRIP, TOK), 1)
    masks = []
    for a in range(STRIPS):
        part = mask[a * STRIP:(a + 1) * STRIP, TOK:]
        shift = TOK - STRIP - a * STRIP
        if shift:
            part = jnp.where(lane >= shift, pltpu.roll(part, shift, 1), 0.0)
        masks.append(part.astype(bf16))

    def build_modal(g, c):
        row = jnp.broadcast_to(hline[pl.ds(g, 1), :], (STRIP, TOK))
        base = pltpu.roll(row, 0, 1, stride=1, stride_axis=0).astype(bf16)
        at = pl.ds(pl.multiple_of((g & 15) * STRIP, STRIP), STRIP)
        for a in range(STRIPS):
            modal[(g >> 4) * STRIPS + a, at, :] = base * masks[a]
        return c

    lax.fori_loop(0, GROUPS, build_modal, 0, unroll=16)

    tile = one_hot((iota((MODES, GROUPS * MODES), 1) & 15) == iota((MODES, GROUPS * MODES), 0))
    own_group = half + (iota((PAIR, GROUPS * MODES), 1) >> 4) == iota((PAIR, GROUPS * MODES), 0)

    def as_row(per_group):
        spread = jnp.where(own_group, dot(per_group.astype(bf16), tile), 0.0)
        return jnp.sum(spread, axis=0, keepdims=True)

    rate_row = as_row(rate16)
    scaled_row = scaled_of(rate_row, as_row(res16))
    steps = (iota((TOK, 1), 0) + 1).astype(f32)
    carry[...] = (jnp.exp(-rate_row * steps) * scaled_row * continues).astype(bf16)

    @pl.when(is_mediator)
    def _():
        group_of = half + med_block * GB + (iota((PAIR, LANES), 1) >> 4)
        rates = dot_rows(rate16.astype(bf16), one_hot(group_of == iota((PAIR, LANES), 0)))
        decay[...] = jnp.exp(-rates * TOK)
        no_start[...] = jnp.broadcast_to(
            jnp.where(jnp.sum(starts[...], axis=1, keepdims=True) == 0, 1.0, 0.0), (CTX, LANES)
        )

    @pl.when(cx == 0)
    def _():
        states[...] = jnp.zeros((NB, MODES, LANES), bf16)

    same_group = one_hot((iota((LANES, LANES), 0) >> 4) == (iota((LANES, LANES), 1) >> 4))
    for j in range(NB):
        value = gated[j, TOK - STRIP:, :]
        inside = jnp.concatenate(
            [pick(dot(modal[j * STRIPS + a], gated[j, a * STRIP:a * STRIP + TOK, :]), STRIP) for a in range(STRIPS)], axis=0
        )
        partial[j] = inside + skip[:, j * LANES:(j + 1) * LANES] * value.astype(f32)

    @pl.when(is_mediator)
    def _():
        def return_one(to, c):
            @pl.when(to != cx)
            def _():
                pltpu.make_async_remote_copy(
                    prefix.at[to], states.at[med_block], p2_send, p2_recv.at[med_block],
                    device_id=(fs, to, dp), device_id_type=MESH,
                ).start()

            @pl.when(to == cx)
            def _():
                pltpu.make_async_copy(prefix.at[to], states.at[med_block], p2_recv.at[med_block]).start()

            return c

        total_state = jnp.zeros((MODES, LANES), f32)
        for part in range(CTX // PART):
            rows = pl.ds(part * PART, PART)
            pltpu.make_async_copy(recv.at[rows], recv.at[rows], p1_recv.at[part]).wait()
            last = min((part + 1) * PART, CTX - 1)
            for p in range(part * PART, last):
                total_state = total_state * (decay[...] * no_start[pl.ds(p, 1), :]) + recv[p].astype(f32)
                prefix[p + 1] = total_state.astype(bf16)
            if last % ROW == 0:
                return_one(last, 0)
            opens = part * PART % ROW == 0
            lax.fori_loop(part * PART + opens, (part + 1) * PART, return_one, 0)

    for j in range(NB):
        @pl.when(cx > 0)
        def _():
            pltpu.make_async_copy(states.at[j], states.at[j], p2_recv.at[j]).wait()

        spread = jnp.concatenate([states[j]] * GB, axis=0) * same_group
        carried = dot(carry[:, j * LANES:(j + 1) * LANES], spread)
        out[0, :, j * LANES:(j + 1) * LANES] = (partial[j] + carried).astype(bf16)

    @pl.when(cx < CTX - 1)
    def _():
        for halo in halos:
            halo.wait_send()

    for j in range(NB):
        @pl.when(cx != j * ROW)
        def _():
            pltpu.make_async_copy(e_buf.at[j], e_buf.at[j], p1_send.at[j]).wait()

    @pl.when(is_mediator)
    def _():
        def drain(i, c):
            pltpu.make_async_copy(prefix.at[0], prefix.at[0], p2_send).wait()
            return c

        lax.fori_loop(0, jnp.where(cx == 0, CTX - 1, CTX - 2), drain, 0)


def body(query, key, value, starts, taps, rate, residue, skip):
    any_space = pl.BlockSpec(memory_space=pltpu.MemorySpace.HBM)
    vmem = pl.BlockSpec(memory_space=pltpu.VMEM)
    dma = pltpu.SemaphoreType.DMA
    return pl.pallas_call(
        kernel,
        out_shape=pltpu.VMEM((1, TOK, WIDE), bf16),
        in_specs=[any_space] * 3 + [vmem] + [any_space] * 3 + [vmem],
        out_specs=vmem,
        scratch_shapes=[
            pltpu.VMEM((TOK, WIDE), bf16),
            pltpu.VMEM((TOK, WIDE), bf16),
            pltpu.VMEM((TOK, WIDE), bf16),
            pltpu.VMEM((NB, 3 * TOK, LANES), bf16),
            pltpu.VMEM((2, TOK // 2, PAIR), bf16),
            pltpu.VMEM((4, 4, PAIR), bf16),
            pltpu.VMEM((4, 4, PAIR), bf16),
            pltpu.VMEM((PAIR, 2 * TOK), f32),
            pltpu.VMEM((GROUPS, TOK), f32),
            pltpu.VMEM((NB * STRIPS, GB * STRIP, 2 * TOK), bf16),
            pltpu.VMEM((NB * STRIPS, GB * STRIP, TOK), bf16),
            pltpu.VMEM((GROUPS * MODES, TOK), bf16),
            pltpu.VMEM((TOK, GROUPS * MODES), bf16),
            pltpu.VMEM((NB, 2 * TOK - STRIP, LANES), bf16),
            pltpu.VMEM((NB, TOK, LANES), f32),
            pltpu.VMEM((NB, MODES, LANES), bf16),
            pltpu.VMEM((CTX, MODES, LANES), bf16),
            pltpu.VMEM((CTX, MODES, LANES), bf16),
            pltpu.VMEM((NB, MODES, LANES), bf16),
            pltpu.VMEM((MODES, LANES), f32),
            pltpu.VMEM((CTX, LANES), f32),
            pltpu.VMEM((GROUPS * MODES, TOK), f32),
            dma((6,)), dma((NB,)), dma((NB,)), dma, dma, dma((2, 3)), dma((2, 3)),
            dma((NB,)), dma((CTX // PART,)), dma, dma((NB,)),
        ],
        compiler_params=pltpu.CompilerParams(
            collective_id=1, has_side_effects=True, vmem_limit_bytes=60000000
        ),
    )(query, key, value, starts.reshape(CTX, TOK), taps.T, rate.T, residue.T, skip.reshape(1, WIDE))


def solution(mesh):
    return jax.shard_map(
        body,
        mesh=mesh,
        in_specs=(
            P(None, "ctx", ("fsdp", "dp")),
            P(None, "ctx", ("fsdp", "dp")),
            P(None, "ctx", ("fsdp", "dp")),
            P(),
            P(None, "fsdp"),
            P("fsdp", "dp"),
            P("fsdp", "dp"),
            P(("fsdp", "dp")),
        ),
        out_specs=P(None, "ctx", ("fsdp", "dp")),
        check_vma=False,
    )
```

```python
import functools

import jax
import jax.numpy as jnp
from jax import lax
from jax.experimental import pallas as pl
from jax.experimental.pallas import tpu as pltpu
from jax.sharding import PartitionSpec as P

MESH = pl.DeviceIdType.MESH
CH = 16
MODES = 16
TOK = 128
LANES = 256
GB = LANES // CH
NB = 4
WIDE = NB * LANES
GROUPS = WIDE // CH
PAIR = 2 * GROUPS
CTX = 64
ROW = 16
PART = 8
STRIP = 16
STRIPS = TOK // STRIP

f32 = jnp.float32
bf16 = jnp.bfloat16


def iota(shape, dim):
    return lax.broadcasted_iota(jnp.int32, shape, dim)


def one_hot(cond):
    return jnp.where(cond, 1.0, 0.0).astype(bf16)


def dot(a, b):
    return jnp.dot(a, b, preferred_element_type=f32)


def dot_rows(a, b):
    return lax.dot_general(a, b, (((0,), (0,)), ((), ())), preferred_element_type=f32)


def minus_expm1_neg(x):
    series = x * (1.0 - x * (0.5 - x * (1.0 / 6 - x * (1.0 / 24 - x * (1.0 / 120 - x * (1.0 / 720))))))
    return jnp.where(x < 0.125, series, 1.0 - jnp.exp(-x))


def scaled_of(rate, residue):
    return residue * jnp.sqrt(minus_expm1_neg(2.0 * rate) * (1.0 / MODES))


def kernel(
    q_hbm, k_hbm, v_hbm, starts, taps_hbm, rate_hbm, residue_hbm, skip, out,
    q_buf, k_buf, v_buf, window, tapbuf, ratebuf, resbuf, line, hline, toep, modal, ends, carry,
    gated, partial, e_buf, recv, prefix, states, decay, no_start, powers_buf,
    in_sem, halo_send, halo_recv, tap_send, tap_recv, mod_send, mod_recv, p1_send, p1_recv, p2_send, p2_recv,
):
    fs = lax.axis_index("fsdp")
    cx = lax.axis_index("ctx")
    dp = lax.axis_index("dp")

    loads = [
        pltpu.make_async_copy(k_hbm.at[0], k_buf, in_sem.at[0]),
        pltpu.make_async_copy(v_hbm.at[0], v_buf, in_sem.at[1]),
        pltpu.make_async_copy(q_hbm.at[0], q_buf, in_sem.at[2]),
    ]
    for load in loads:
        load.start()

    is_mediator = lax.rem(cx, ROW) == 0
    med_block = cx // ROW
    part_of = cx // PART

    barrier = pltpu.get_barrier_semaphore()

    @pl.when(cx > 0)
    def _():
        pl.semaphore_signal(barrier, inc=1, device_id=(fs, cx - 1, dp), device_id_type=MESH)

    pl.semaphore_signal(barrier, inc=1, device_id=(1 - fs, cx, dp), device_id_type=MESH)
    for d in (1, 2, 3):
        pl.semaphore_signal(
            barrier, inc=1, device_id=(fs, cx, lax.rem(dp + d, 4)), device_id_type=MESH
        )

    @pl.when(is_mediator)
    def _():
        def greet(d, c):
            pl.semaphore_signal(
                barrier, inc=1, device_id=(fs, lax.rem(cx + d, CTX), dp), device_id_type=MESH
            )
            return c

        lax.fori_loop(1, CTX, greet, 0)

    own_row = starts[pl.ds(cx, 1), :].astype(f32)
    before_row = starts[pl.ds(lax.rem(cx + CTX - 1, CTX), 1), :].astype(f32)
    both = jnp.concatenate([before_row, own_row], axis=1)
    t_of = iota((TOK, 2 * TOK), 0)
    s_of = iota((TOK, 2 * TOK), 1)
    at_row = jnp.sum(jnp.where(s_of <= t_of + TOK, both, 0.0), axis=1, keepdims=True)
    upper = one_hot(iota((2 * TOK, 2 * TOK), 0) <= iota((2 * TOK, 2 * TOK), 1))
    counts = dot(jnp.broadcast_to(both, (8, 2 * TOK)).astype(bf16), upper)[0:1]
    first = jnp.where(cx == 0, TOK, 0)
    mask = jnp.where((at_row == counts) & (s_of <= t_of + TOK) & (s_of >= first), 1.0, 0.0)
    before = jnp.sum(before_row, axis=1, keepdims=True)
    total = before + jnp.sum(own_row, axis=1, keepdims=True)
    keep = jnp.where(counts[:, TOK:] == total, 1.0, 0.0)
    continues = jnp.where(at_row == before, 1.0, 0.0)

    loads[0].wait()
    loads[1].wait()
    for j in range(NB):
        cols = pl.ds(j * LANES, LANES)
        window[j, TOK:2 * TOK, :] = (k_buf[:, cols].astype(f32) * v_buf[:, cols].astype(f32)).astype(bf16)
        window[j, 2 * TOK:, :] = jnp.zeros((TOK, LANES), bf16)
        gated[j, :TOK - STRIP, :] = jnp.zeros((TOK - STRIP, LANES), bf16)

    @pl.when(cx == 0)
    def _():
        for j in range(NB):
            window[j, :TOK, :] = jnp.zeros((TOK, LANES), bf16)

    pl.semaphore_wait(barrier, NB + 4 - jnp.where(is_mediator, 1, 0) + jnp.where(cx < CTX - 1, 1, 0))

    def order(row):
        return [lax.rem(row + d, NB) for d in (2, 3, 1, 0)]

    def halo_copies(row):
        return [
            pltpu.make_async_remote_copy(
                window.at[j, pl.ds(TOK, TOK)], window.at[j, pl.ds(0, TOK)], halo_send.at[j], halo_recv.at[j],
                device_id=(fs, lax.rem(cx + 1, CTX), dp), device_id_type=MESH,
            )
            for j in order(row)
        ]

    halos = halo_copies(lax.rem(cx + 1, CTX) // ROW)
    arriving = halo_copies(med_block)

    @pl.when(cx < CTX - 1)
    def _():
        for halo in halos:
            halo.start()

    half = lax.rem(dp, 2) * GROUPS
    other = pl.multiple_of(((1 - fs) * 2 + dp // 2) * PAIR, PAIR)
    mine = pl.multiple_of((fs * 2 + dp // 2) * PAIR, PAIR)
    tap_copy = pltpu.make_async_remote_copy(
        taps_hbm.at[:, pl.ds(other, PAIR)], tapbuf.at[fs], tap_send, tap_recv,
        device_id=(1 - fs, cx, dp), device_id_type=MESH,
    )
    tap_copy.start()
    tap_own = pltpu.make_async_copy(taps_hbm.at[:, pl.ds(mine, PAIR)], tapbuf.at[fs], in_sem.at[3])
    tap_own.start()
    modal_copies = []
    for d in (1, 2, 3):
        to = lax.rem(dp + d, 4)
        pair = pl.ds(pl.multiple_of(to // 2 * PAIR, PAIR), PAIR)
        for i, (src, dst) in enumerate(((rate_hbm, ratebuf), (residue_hbm, resbuf))):
            copy = pltpu.make_async_remote_copy(
                src.at[:, pair], dst.at[dp], mod_send.at[i, d - 1], mod_recv.at[i, d - 1],
                device_id=(fs, cx, to), device_id_type=MESH,
            )
            copy.start()
            modal_copies.append(copy)
    pair = pl.ds(pl.multiple_of(dp // 2 * PAIR, PAIR), PAIR)
    rate_own = pltpu.make_async_copy(rate_hbm.at[:, pair], ratebuf.at[dp], in_sem.at[4])
    residue_own = pltpu.make_async_copy(residue_hbm.at[:, pair], resbuf.at[dp], in_sem.at[5])
    rate_own.start()
    residue_own.start()

    tap_own.wait()
    tap_copy.wait()
    flip = [one_hot(iota((TOK // 2, 2 * TOK), 1) == TOK - h * (TOK // 2) - iota((TOK // 2, 2 * TOK), 0)) for h in (0, 1)]
    line[...] = dot_rows(tapbuf[0], flip[0]) + dot_rows(tapbuf[1], flip[1])

    wide_lane = iota((STRIP, 2 * TOK), 1)
    wide_masks = []
    for a in range(STRIPS):
        part = mask[a * STRIP:(a + 1) * STRIP]
        if a:
            part = pltpu.roll(part, 2 * TOK - a * STRIP, 1)
        wide_masks.append(jnp.where(wide_lane < TOK + STRIP, part, 0.0).astype(bf16))

    def build_medium(g, c):
        row = jnp.broadcast_to(line[pl.ds(half + g, 1), :], (STRIP, 2 * TOK))
        base = pltpu.roll(row, 0, 1, stride=1, stride_axis=0).astype(bf16)
        at = pl.ds(pl.multiple_of((g & 15) * STRIP, STRIP), STRIP)
        for a in range(STRIPS):
            toep[(g >> 4) * STRIPS + a, at, :] = base * wide_masks[a]
        return c

    lax.fori_loop(0, GROUPS, build_medium, 0, unroll=16)

    rate_own.wait()
    residue_own.wait()
    for copy in modal_copies:
        copy.wait()

    def gather_modes(buf):
        parts = [dot_rows(buf[d], one_hot(iota((4, MODES), 1) == 4 * d + iota((4, MODES), 0))) for d in range(4)]
        return (parts[0] + parts[1]) + (parts[2] + parts[3])

    rate16 = gather_modes(ratebuf)
    res16 = gather_modes(resbuf)
    repeat = one_hot(half + (iota((GROUPS * MODES, PAIR), 0) >> 4) == iota((GROUPS * MODES, PAIR), 1))
    own_mode = (iota((GROUPS * MODES, MODES), 0) & 15) == iota((GROUPS * MODES, MODES), 1)
    ones = jnp.ones((MODES, TOK), bf16)

    def column(per_group):
        spread = jnp.where(own_mode, dot(repeat, per_group.astype(bf16)), 0.0)
        return dot(spread.astype(bf16), ones)

    rate_col = column(rate16)
    lag = ((TOK - STRIP - iota((1, TOK), 1)) & (TOK - 1)).astype(f32)
    powers = jnp.exp(-rate_col * lag)
    powers_buf[...] = powers
    ends[...] = (pltpu.roll(powers, STRIP - 1, 1) * keep).astype(bf16)

    loads[2].wait()
    lane_group = iota((1, LANES), 1) >> 4

    def pick(rows, size):
        out_rows = rows[:size]
        for i in range(1, GB):
            out_rows = jnp.where(lane_group == i, rows[i * size:(i + 1) * size], out_rows)
        return out_rows

    for i, j in enumerate(order(med_block)):
        @pl.when(cx > 0)
        def _():
            arriving[i].wait_recv()

        medium = jnp.concatenate(
            [pick(dot(toep[j * STRIPS + a], window[j, a * STRIP:a * STRIP + 2 * TOK, :]), STRIP) for a in range(STRIPS)], axis=0
        )
        value = (q_buf[:, pl.ds(pl.multiple_of(j * LANES, LANES), LANES)].astype(f32) * medium.astype(bf16).astype(f32)).astype(bf16)
        gated[j, TOK - STRIP:, :] = value
        full = dot(ends[pl.ds(pl.multiple_of(j * GB * MODES, GB * MODES), GB * MODES), :], value)
        e_buf[j] = pick(full, MODES).astype(bf16)

        @pl.when(cx != j * ROW)
        def _():
            pltpu.make_async_remote_copy(
                e_buf.at[j], recv.at[cx], p1_send.at[j], p1_recv.at[part_of],
                device_id=(fs, j * ROW, dp), device_id_type=MESH,
            ).start()

        @pl.when(cx == j * ROW)
        def _():
            pltpu.make_async_copy(e_buf.at[j], recv.at[cx], p1_recv.at[part_of]).start()

    hline[...] = jnp.sum((powers_buf[...] * scaled_of(rate_col, column(res16))).reshape(GROUPS, MODES, TOK), axis=1)
    lane = iota((STRIP, TOK), 1)
    masks = []
    for a in range(STRIPS):
        part = mask[a * STRIP:(a + 1) * STRIP, TOK:]
        shift = TOK - STRIP - a * STRIP
        if shift:
            part = jnp.where(lane >= shift, pltpu.roll(part, shift, 1), 0.0)
        masks.append(part.astype(bf16))

    def build_modal(g, c):
        row = jnp.broadcast_to(hline[pl.ds(g, 1), :], (STRIP, TOK))
        base = pltpu.roll(row, 0, 1, stride=1, stride_axis=0).astype(bf16)
        at = pl.ds(pl.multiple_of((g & 15) * STRIP, STRIP), STRIP)
        for a in range(STRIPS):
            modal[(g >> 4) * STRIPS + a, at, :] = base * masks[a]
        return c

    lax.fori_loop(0, GROUPS, build_modal, 0, unroll=16)

    tile = one_hot((iota((MODES, GROUPS * MODES), 1) & 15) == iota((MODES, GROUPS * MODES), 0))
    own_group = half + (iota((PAIR, GROUPS * MODES), 1) >> 4) == iota((PAIR, GROUPS * MODES), 0)

    def as_row(per_group):
        spread = jnp.where(own_group, dot(per_group.astype(bf16), tile), 0.0)
        return jnp.sum(spread, axis=0, keepdims=True)

    rate_row = as_row(rate16)
    scaled_row = scaled_of(rate_row, as_row(res16))
    steps = (iota((TOK, 1), 0) + 1).astype(f32)
    carry[...] = (jnp.exp(-rate_row * steps) * scaled_row * continues).astype(bf16)

    @pl.when(is_mediator)
    def _():
        group_of = half + med_block * GB + (iota((PAIR, LANES), 1) >> 4)
        rates = dot_rows(rate16.astype(bf16), one_hot(group_of == iota((PAIR, LANES), 0)))
        decay[...] = jnp.exp(-rates * TOK)
        no_start[...] = jnp.broadcast_to(
            jnp.where(jnp.sum(starts[...], axis=1, keepdims=True) == 0, 1.0, 0.0), (CTX, LANES)
        )

    @pl.when(cx == 0)
    def _():
        states[...] = jnp.zeros((NB, MODES, LANES), bf16)

    same_group = one_hot((iota((LANES, LANES), 0) >> 4) == (iota((LANES, LANES), 1) >> 4))
    for j in range(NB):
        value = gated[j, TOK - STRIP:, :]
        inside = jnp.concatenate(
            [pick(dot(modal[j * STRIPS + a], gated[j, a * STRIP:a * STRIP + TOK, :]), STRIP) for a in range(STRIPS)], axis=0
        )
        partial[j] = inside + skip[:, j * LANES:(j + 1) * LANES] * value.astype(f32)

    def finish(waits=True):
        for j in range(NB):
            if waits:
                pltpu.make_async_copy(states.at[j], states.at[j], p2_recv.at[j]).wait()
            spread = jnp.concatenate([states[j]] * GB, axis=0) * same_group
            carried = dot(carry[:, j * LANES:(j + 1) * LANES], spread)
            out[0, :, j * LANES:(j + 1) * LANES] = (partial[j] + carried).astype(bf16)

    @pl.when(cx == 0)
    def _():
        finish(waits=False)

    @pl.when(is_mediator)
    def _():
        def return_one(to, c):
            @pl.when(to != cx)
            def _():
                pltpu.make_async_remote_copy(
                    prefix.at[to], states.at[med_block], p2_send, p2_recv.at[med_block],
                    device_id=(fs, to, dp), device_id_type=MESH,
                ).start()

            @pl.when(to == cx)
            def _():
                pltpu.make_async_copy(prefix.at[to], states.at[med_block], p2_recv.at[med_block]).start()

            return c

        total_state = jnp.zeros((MODES, LANES), f32)
        for part in range(CTX // PART):
            rows = pl.ds(part * PART, PART)
            pltpu.make_async_copy(recv.at[rows], recv.at[rows], p1_recv.at[part]).wait()
            last = min((part + 1) * PART, CTX - 1)
            for p in range(part * PART, last):
                total_state = total_state * (decay[...] * no_start[pl.ds(p, 1), :]) + recv[p].astype(f32)
                prefix[p + 1] = total_state.astype(bf16)
            if last % ROW == 0:
                return_one(last, 0)
            opens = part * PART % ROW == 0
            lax.fori_loop(part * PART + opens, (part + 1) * PART, return_one, 0)
            if (part + 1) * PART % ROW == 0 and part * PART >= ROW:
                @pl.when(med_block == part * PART // ROW)
                def _():
                    finish()

    @pl.when(jnp.logical_not(is_mediator))
    def _():
        finish()

    @pl.when(cx < CTX - 1)
    def _():
        for halo in halos:
            halo.wait_send()

    for j in range(NB):
        @pl.when(cx != j * ROW)
        def _():
            pltpu.make_async_copy(e_buf.at[j], e_buf.at[j], p1_send.at[j]).wait()

    @pl.when(is_mediator)
    def _():
        def drain(i, c):
            pltpu.make_async_copy(prefix.at[0], prefix.at[0], p2_send).wait()
            return c

        lax.fori_loop(0, jnp.where(cx == 0, CTX - 1, CTX - 2), drain, 0)


def body(query, key, value, starts, taps, rate, residue, skip):
    any_space = pl.BlockSpec(memory_space=pltpu.MemorySpace.HBM)
    vmem = pl.BlockSpec(memory_space=pltpu.VMEM)
    dma = pltpu.SemaphoreType.DMA
    return pl.pallas_call(
        kernel,
        out_shape=pltpu.VMEM((1, TOK, WIDE), bf16),
        in_specs=[any_space] * 3 + [vmem] + [any_space] * 3 + [vmem],
        out_specs=vmem,
        scratch_shapes=[
            pltpu.VMEM((TOK, WIDE), bf16),
            pltpu.VMEM((TOK, WIDE), bf16),
            pltpu.VMEM((TOK, WIDE), bf16),
            pltpu.VMEM((NB, 3 * TOK, LANES), bf16),
            pltpu.VMEM((2, TOK // 2, PAIR), bf16),
            pltpu.VMEM((4, 4, PAIR), bf16),
            pltpu.VMEM((4, 4, PAIR), bf16),
            pltpu.VMEM((PAIR, 2 * TOK), f32),
            pltpu.VMEM((GROUPS, TOK), f32),
            pltpu.VMEM((NB * STRIPS, GB * STRIP, 2 * TOK), bf16),
            pltpu.VMEM((NB * STRIPS, GB * STRIP, TOK), bf16),
            pltpu.VMEM((GROUPS * MODES, TOK), bf16),
            pltpu.VMEM((TOK, GROUPS * MODES), bf16),
            pltpu.VMEM((NB, 2 * TOK - STRIP, LANES), bf16),
            pltpu.VMEM((NB, TOK, LANES), f32),
            pltpu.VMEM((NB, MODES, LANES), bf16),
            pltpu.VMEM((CTX, MODES, LANES), bf16),
            pltpu.VMEM((CTX, MODES, LANES), bf16),
            pltpu.VMEM((NB, MODES, LANES), bf16),
            pltpu.VMEM((MODES, LANES), f32),
            pltpu.VMEM((CTX, LANES), f32),
            pltpu.VMEM((GROUPS * MODES, TOK), f32),
            dma((6,)), dma((NB,)), dma((NB,)), dma, dma, dma((2, 3)), dma((2, 3)),
            dma((NB,)), dma((CTX // PART,)), dma, dma((NB,)),
        ],
        compiler_params=pltpu.CompilerParams(
            collective_id=1, has_side_effects=True, vmem_limit_bytes=60000000
        ),
    )(query, key, value, starts.reshape(CTX, TOK), taps.T, rate.T, residue.T, skip.reshape(1, WIDE))


def solution(mesh):
    return jax.shard_map(
        body,
        mesh=mesh,
        in_specs=(
            P(None, "ctx", ("fsdp", "dp")),
            P(None, "ctx", ("fsdp", "dp")),
            P(None, "ctx", ("fsdp", "dp")),
            P(),
            P(None, "fsdp"),
            P("fsdp", "dp"),
            P("fsdp", "dp"),
            P(("fsdp", "dp")),
        ),
        out_specs=P(None, "ctx", ("fsdp", "dp")),
        check_vma=False,
    )
```
